256 devices in a mesh: dp: 32 (over z, x_lo, core), tp: 8 (over x_hi, y).
Axes of the slice: x: 4 (x_hi: 2, x_lo: 2; x = x_hi * 2 + x_lo), y: 4, z: 8, core: 2. Of those that a mesh axis runs over, the one named last changes fastest.
Arguments:
- queries: bfloat16 [256, 8192], P('dp', 'tp'), may hold values from -5 to 5
- prefix_kv: bfloat16 [2, 65536, 1024], P(None, 'dp', 'tp'), may hold values from -5 to 5
- cache_kv: bfloat16 [2, 2048, 64, 1024], P(None, 'dp', None, 'tp'), may hold values from -5 to 5
- lengths: int32 [256], P('dp'), may hold values from 1 to 512, as said below
- page_table: int32 [32, 64], P('dp'), may hold values from 0 to 63, each once within a row
- owner: int32 [32], replicated, may hold values from 0 to 31, as said below
- readers: int32 [16], replicated, may hold values from 0 to 31, as said below
- w_out: bfloat16 [8192, 4096], P('tp'), may hold values from -0.5 to 0.5
Outputs:
- projected: bfloat16 [256, 4096], P('dp', 'tp')
The draws below stay inside these ranges and needn't reach their ends.
Inputs may be any that keep to these rules, and one draw needn't show every extreme that they name: `lengths`: at most 512, reached by some request in every draw. `page_table`: each row holds every page id of its replica once. `owner`: every replica index once. `readers`: 16 distinct replica indices, none of them owner[0].
All inputs are finite; a program needn't handle non-finite values.
Results may differ from the reference program's by a relative error of at most 0.0051.
Values may be sent and summed in bfloat16 or wider, within the bound.
A program may use at most 64 MiB of HBM per device.

```python
import jax
import jax.numpy as jnp
from jax import lax

HEADS = 64
KV_HEADS = 8
HD = 128
D_OUT = 4096
PREFIX = 2048
PAGE = 64
MAXLEN = 512
B = 8
NPAGES = 64
READERS = 16
N_DP = 32


def draw_queries(key, part):
    rows = N_DP * B
    values = jnp.clip(2.0 * jax.random.normal(jax.random.fold_in(key, 23), (rows, HEADS, HD), jnp.float32), -5.0, 5.0)
    return values.reshape(rows, HEADS * HD).astype(jnp.bfloat16)


def draw_cache_kv(key, part):
    shape = (2, N_DP * NPAGES, PAGE, KV_HEADS, HD)
    values = jnp.clip(jax.random.normal(jax.random.fold_in(key, 32), shape, jnp.float32), -5.0, 5.0)
    return values.reshape(2, N_DP * NPAGES, PAGE, KV_HEADS * HD).astype(jnp.bfloat16)


def draw_lengths(key, part):
    caps = jax.random.randint(jax.random.fold_in(key, 41), (N_DP, 1), MAXLEN // 4, MAXLEN + 1)
    raw = jax.random.randint(jax.random.fold_in(key, 42), (N_DP, B), 0, 1 << 20)
    lens = 1 + raw % caps
    chosen = jax.random.randint(jax.random.fold_in(key, 43), (), 0, N_DP)
    lens = lens.at[chosen, 0].set(MAXLEN)
    return lens.reshape(N_DP * B).astype(jnp.int32)


def owner_and_readers(key):
    ranking = jax.random.permutation(jax.random.fold_in(key, 61), N_DP).astype(jnp.int32)
    first = ranking[0]
    offsets = jnp.arange(1, N_DP, dtype=jnp.int32)
    tier = jnp.where(offsets == 1, 3, jnp.where(offsets == N_DP // 2, 2, jnp.where(offsets == N_DP - 1, 1, 0)))
    noise = jax.random.randint(jax.random.fold_in(key, 62), (N_DP - 1,), 0, 1024)
    scores = (tier * 1024 + noise) * N_DP + offsets
    _, picked = lax.top_k(scores, READERS)
    chosen = offsets[picked]
    readers = (first + chosen) % N_DP
    return (ranking, readers.astype(jnp.int32))


def draw_owner(key, part):
    return owner_and_readers(key)[0]


def draw_readers(key, part):
    return owner_and_readers(key)[1]


def with_spikes(values, stream_key, source, target, blocks, factor):
    def block_of(dim):
        return (jnp.arange(values.shape[dim]) // (values.shape[dim] // blocks)).reshape((-1,) + (1,) * (values.ndim - 1 - dim))

    one_side = jax.random.permutation(stream_key, blocks)[block_of(target)]
    other_side = (block_of(target) + blocks // 2) % blocks
    return jnp.where((block_of(source) == one_side) | (block_of(source) == other_side), factor * values, values)


def steps_of(rng, extent, shards, least, high):
    factor_of = 1.0
    for position, blocks in shards:
        heights = jax.random.uniform(jax.random.fold_in(jax.random.fold_in(rng, 6), position), (blocks,), jnp.float32, least / len(shards), high / len(shards))
        factor_of = factor_of * jnp.repeat(jnp.exp(heights), extent[position] // blocks).reshape((-1,) + (1,) * (len(extent) - 1 - position))
    return factor_of


def normal_values(own_key, extent, deviation, reach, shards=(), kind=jnp.bfloat16):
    result = deviation * jax.random.normal(own_key, extent, jnp.float32)
    if shards:
        result = result * steps_of(own_key, extent, shards, -0.22, 0.18)
    return jnp.clip(result, -reach, reach).astype(kind)


def bell_draw_with(key, dims, spread, limit, split, heavy, held_as=jnp.bfloat16):
    values = spread * jax.random.normal(key, dims, jnp.float32)
    if split:
        values = values * steps_of(key, dims, split, -0.22, 0.18)
    return jnp.clip(with_spikes(values, jax.random.fold_in(key, 3), *heavy), -limit, limit).astype(held_as)


def setup_inputs(seed: int = 0) -> dict:
    key_list = jax.random.split(jax.random.key(seed), 9)
    return {
        "queries": draw_queries(jax.random.fold_in(key_list[8], 71), 0),
        "prefix_kv": normal_values(key_list[1], (2, N_DP * PREFIX, KV_HEADS * HD), 1.0, 5.0, ((1, 32), (2, 8))),
        "cache_kv": draw_cache_kv(jax.random.fold_in(key_list[8], 71), 0),
        "lengths": draw_lengths(jax.random.fold_in(key_list[8], 71), 0),
        "page_table": jax.vmap(lambda own: jax.random.permutation(own, NPAGES))(jax.random.split(key_list[4], N_DP)).reshape((N_DP, NPAGES)).astype(jnp.int32),
        "owner": draw_owner(jax.random.fold_in(key_list[8], 71), 0),
        "readers": draw_readers(jax.random.fold_in(key_list[8], 71), 0),
        "w_out": bell_draw_with(key_list[7], (HEADS * HD, D_OUT), 0.08, 0.5, ((0, 8),), (0, 1, 8, 2.0)),
    }


def reference(queries, prefix_kv, cache_kv, lengths, page_table, owner, readers, w_out):
    group = HEADS // KV_HEADS
    maxpages = MAXLEN // PAGE
    scale = 1.0 / (HD ** 0.5)
    start = (owner[0] * PREFIX).astype(jnp.int32)
    prefix = lax.dynamic_slice_in_dim(prefix_kv, start, PREFIX, 1)
    prefix = prefix.reshape(2, PREFIX, KV_HEADS, HD).astype(jnp.float32)
    replicas = jnp.arange(N_DP, dtype=jnp.int32)
    flags = jnp.any(readers[None, :] == replicas[:, None], axis=1)

    def replica(index):
        first = (index * B).astype(jnp.int32)
        query = lax.dynamic_slice_in_dim(queries, first, B, 0)
        query = query.reshape(B, KV_HEADS, group, HD).astype(jnp.float32)
        pages = page_table[index].reshape(B, maxpages) + index * NPAGES
        resident = cache_kv[:, pages].reshape(2, B, MAXLEN, KV_HEADS, HD).astype(jnp.float32)
        lens = lax.dynamic_slice_in_dim(lengths, first, B, 0)
        s_res = jnp.einsum("bkgd,btkd->bkgt", query, resident[0]) * scale
        inside = jnp.arange(MAXLEN, dtype=jnp.int32)[None, :] < lens[:, None]
        s_res = jnp.where(inside[:, None, None, :], s_res, -jnp.inf)
        s_pre = jnp.einsum("bkgd,tkd->bkgt", query, prefix[0]) * scale
        s_pre = jnp.where(flags[index], s_pre, -jnp.inf)
        top = jnp.maximum(jnp.max(s_res, axis=-1), jnp.max(s_pre, axis=-1))
        e_res = jnp.exp(s_res - top[..., None])
        e_pre = jnp.exp(s_pre - top[..., None])
        den = jnp.sum(e_res, axis=-1) + jnp.sum(e_pre, axis=-1)
        r_res = lax.optimization_barrier(e_res.astype(jnp.bfloat16)).astype(jnp.float32)
        r_pre = lax.optimization_barrier(e_pre.astype(jnp.bfloat16)).astype(jnp.float32)
        num = jnp.einsum("bkgt,btkd->bkgd", r_res, resident[1]) + jnp.einsum("bkgt,tkd->bkgd", r_pre, prefix[1])
        return (num / den[..., None]).astype(jnp.bfloat16).reshape(B, HEADS * HD)

    attn = lax.map(replica, replicas).reshape(N_DP * B, HEADS * HD)
    return jnp.dot(attn, w_out, preferred_element_type=jnp.float32).astype(jnp.bfloat16)
```

```python
import functools
import math

import jax
import jax.numpy as jnp
from jax import lax
from jax.experimental import pallas as pl
from jax.experimental.pallas import tpu as pltpu
from jax.sharding import PartitionSpec as P

HD = 128
MESH = pl.DeviceIdType.MESH
LOG2E = math.log2(math.e)
LOW = -1e30
NZ, NX, NC, NY, NXH = 8, 2, 2, 4, 2
TP_STEPS = sorted(
    [(kx, ky) for kx in range(NXH) for ky in range(NY) if kx or ky],
    key=lambda k: -(2 * k[0] + min(k[1], NY - k[1])),
)


def nt_dot(a, b):
    return lax.dot_general(
        a, b, (((1,), (1,)), ((), ())), preferred_element_type=jnp.float32
    )


def kernel(
    oz,
    ox,
    lens_ref,
    table_ref,
    owner_ref,
    readers_ref,
    q_hbm,
    prefix_hbm,
    cache_hbm,
    w_hbm,
    out_ref,
    q_in,
    q_f32,
    q_rows,
    cache,
    kv,
    w,
    q_buf,
    o_send,
    s_send,
    o_recv,
    s_recv,
    num_res,
    ml_res,
    attn_f32,
    lse_f32,
    part_send,
    part_recv,
    local_sem,
    kv_send,
    kv_recv,
    q_send_sem,
    q_recv_sem,
    o_send_sem,
    s_send_sem,
    o_recv_sem,
    s_recv_sem,
    p_send_sem,
    p_recv_sem,
):
    dp, tp = lax.axis_index("dp"), lax.axis_index("tp")
    z, x, c = dp // 4, (dp // 2) % 2, dp % 2
    xh, y = tp // NY, tp % NY
    dz, dx = (z + NZ - oz) % NZ, (x + NX - ox) % NX
    here = dz * 2 + dx
    at_owner = here == 0
    rows = q_in.shape[0]
    heads = q_in.shape[1] // HD
    n = rows * heads
    pages, page = cache.shape[1], cache.shape[2]
    per = pages // rows
    c2 = LOG2E / HD**0.5

    def at(zz, xx, cc):
        return (zz * 4 + xx * 2 + cc, tp)

    def tp_peer(kx, ky):
        return (dp, ((xh + kx) % NXH) * NY + (y + ky) % NY)

    barrier = pltpu.get_barrier_semaphore()
    for k in TP_STEPS:
        pl.semaphore_signal(barrier, 1, device_id=tp_peer(*k), device_id_type=MESH)

    @pl.when(at_owner)
    def _():
        pl.semaphore_signal(barrier, 1, device_id=at(oz, ox, 1 - c), device_id_type=MESH)
        for i in range(2 * NZ - 1, 0, -1):
            pl.semaphore_signal(
                barrier,
                1,
                device_id=at((oz + i // 2) % NZ, (ox + i % 2) % NX, c),
                device_id_type=MESH,
            )

    load_q = pltpu.make_async_copy(q_hbm, q_in, local_sem.at[0])
    load_cache = pltpu.make_async_copy(cache_hbm, cache, local_sem.at[1])
    load_w = pltpu.make_async_copy(w_hbm, w, local_sem.at[2])
    load_kv = pltpu.make_async_copy(prefix_hbm, kv.at[0], local_sem.at[3])
    load_q.start()
    load_cache.start()

    @pl.when(at_owner)
    def _():
        load_kv.start()

    load_w.start()

    load_q.wait()
    for g in range(heads):
        q_f32[pl.ds(g, rows, stride=heads), :] = q_in[:, g * HD : (g + 1) * HD].astype(
            jnp.float32
        )
    q_rows[...] = q_f32[...].astype(jnp.bfloat16)

    def query_copy():
        return pltpu.make_async_remote_copy(
            q_rows,
            q_buf.at[dz, pl.ds(pl.multiple_of(dx * n, n), n)],
            q_send_sem,
            q_recv_sem.at[here],
            device_id=at(oz, ox, c),
            device_id_type=MESH,
        )

    @pl.when(jnp.logical_not(at_owner))
    def _():
        pl.semaphore_wait(barrier, len(TP_STEPS) + 1)
        query_copy().start()

    def kv_copy(i):
        return pltpu.make_async_remote_copy(
            prefix_hbm.at[i],
            kv.at[1, i],
            kv_send.at[i],
            kv_recv.at[i],
            device_id=at(oz, ox, 1 - c),
            device_id_type=MESH,
        )

    load_cache.wait()
    for b in range(rows):
        keys = jnp.concatenate(
            [cache[0, table_ref[0, b * per + j]] for j in range(per)], axis=0
        )
        s = nt_dot(q_f32[b * heads : (b + 1) * heads, :].astype(jnp.bfloat16), keys)
        pos = lax.broadcasted_iota(jnp.int32, s.shape, 1)
        s = jnp.where(pos < lens_ref[b], s, LOW)
        m = jnp.max(s, axis=-1, keepdims=True)
        e = jnp.exp2((s - m) * c2)
        values = jnp.concatenate(
            [cache[1, table_ref[0, b * per + j]] for j in range(per)], axis=0
        )
        here_rows = pl.ds(b * heads, heads)
        ml_res[0, here_rows, :] = jnp.broadcast_to(m * c2, (heads, HD))
        ml_res[1, here_rows, :] = jnp.broadcast_to(
            jnp.sum(e, axis=-1, keepdims=True), (heads, HD)
        )
        num_res[here_rows, :] = jnp.dot(
            e.astype(jnp.bfloat16), values, preferred_element_type=jnp.float32
        )

    @pl.when(at_owner)
    def _():
        pl.semaphore_wait(barrier, len(TP_STEPS) + 1)
        for i in range(2):
            kv_copy(i).start()
        q_buf[0, 0:n, :] = q_rows[...]
        load_kv.wait()
        for i in range(2):
            kv_copy(i).wait()
        source = (owner_ref[0] % NC + c) % 2

        def reply(zz, k, i):
            peer = at((oz + zz) % NZ, (ox + k) % NX, c)
            return (
                pltpu.make_async_remote_copy(
                    o_send.at[zz, pl.ds(k * n, n)],
                    o_recv,
                    o_send_sem.at[i],
                    o_recv_sem,
                    device_id=peer,
                    device_id_type=MESH,
                ),
                pltpu.make_async_remote_copy(
                    s_send.at[zz],
                    s_recv,
                    s_send_sem.at[i],
                    s_recv_sem,
                    device_id=peer,
                    device_id_type=MESH,
                ),
            )

        def arrival(zz, k):
            return pltpu.make_async_remote_copy(
                q_rows,
                q_buf.at[zz, pl.ds(k * n, n)],
                q_send_sem,
                q_recv_sem.at[zz * 2 + k],
                device_id=at(oz, ox, 1 - c),
                device_id_type=MESH,
            )

        def serve(t, carry):
            far = (t + 1) // 2
            zz = (t % 2) * far + (1 - t % 2) * ((NZ - far) % NZ)

            @pl.when(t > 0)
            def _():
                arrival(zz, 0).wait_recv()

            arrival(zz, 1).wait_recv()
            s = nt_dot(q_buf[zz], kv[source, 0])
            m = jnp.max(s, axis=-1, keepdims=True)
            e = jnp.exp2((s - m) * c2)
            total = jnp.sum(e, axis=-1, keepdims=True)
            num = jnp.dot(
                e.astype(jnp.bfloat16), kv[source, 1], preferred_element_type=jnp.float32
            )
            o_send[zz] = (num / total).astype(jnp.bfloat16)
            lse = m * c2 + jnp.log(total) * LOG2E
            s_send[zz] = jnp.transpose(jnp.broadcast_to(lse, (2 * n, HD)))[0:8, :]

            @pl.when(t > 0)
            def _():
                for copy in reply(zz, 0, zz * 2):
                    copy.start()

            for copy in reply(zz, 1, zz * 2 + 1):
                copy.start()
            return carry

        lax.fori_loop(0, NZ, serve, 0)
        o_recv[...] = o_send[0, 0:n, :]
        s_recv[...] = s_send[0]

        def settle(i, carry):
            for copy in reply(0, 0, i):
                copy.wait_send()
            return carry

        lax.fori_loop(1, 2 * NZ, settle, 0)

    @pl.when(jnp.logical_not(at_owner))
    def _():
        query_copy().wait_send()
        pltpu.make_async_remote_copy(
            o_recv, o_recv, o_send_sem.at[0], o_recv_sem, device_id=at(oz, ox, c), device_id_type=MESH
        ).wait_recv()
        pltpu.make_async_remote_copy(
            s_recv, s_recv, s_send_sem.at[0], s_recv_sem, device_id=at(oz, ox, c), device_id_type=MESH
        ).wait_recv()

    reads = readers_ref[0] == dp
    for i in range(1, readers_ref.shape[0]):
        reads = jnp.logical_or(reads, readers_ref[i] == dp)
    lse_f32[...] = jnp.transpose(jnp.broadcast_to(s_recv[0:1, :], (HD, HD)))
    lse = lse_f32[pl.ds(pl.multiple_of(dx * n, n), n), :]
    lse = jnp.where(reads, lse, LOW)
    m_res, l_res = ml_res[0], ml_res[1]
    top = jnp.maximum(m_res, lse)
    w_res, w_pre = jnp.exp2(m_res - top), jnp.exp2(lse - top)
    attn_f32[...] = (num_res[...] * w_res + o_recv[...].astype(jnp.float32) * w_pre) / (
        l_res * w_res + w_pre
    )
    attn = jnp.concatenate(
        [attn_f32[pl.ds(g, rows, stride=heads), :] for g in range(heads)], axis=1
    ).astype(jnp.bfloat16)

    load_w.wait()
    cols = out_ref.shape[1]

    def block(kx, ky):
        start = (((xh + kx) % NXH) * NY + (y + ky) % NY) * cols
        return jnp.dot(
            attn,
            w[:, pl.ds(pl.multiple_of(start, cols), cols)],
            preferred_element_type=jnp.float32,
        )

    def part_copy(kx, ky):
        i = kx * NY + ky
        return pltpu.make_async_remote_copy(
            part_send.at[i],
            part_recv.at[i],
            p_send_sem.at[i],
            p_recv_sem.at[i],
            device_id=tp_peer(kx, ky),
            device_id_type=MESH,
        )

    for k in TP_STEPS:
        part_send[k[0] * NY + k[1]] = block(*k)
        part_copy(*k).start()
    total = block(0, 0)
    for k in TP_STEPS[::-1]:
        part_copy(*k).wait_recv()
        total = total + part_recv[k[0] * NY + k[1]]
    out_ref[...] = total.astype(out_ref.dtype)
    for k in TP_STEPS:
        part_copy(*k).wait_send()


def attend(place, q, prefix, cache, lengths, table, owner, readers, w_out):
    rows, width = q.shape
    n = rows * width // HD
    cols = w_out.shape[1] // (NXH * NY)
    keys = prefix.shape[1]
    bf16, f32 = jnp.bfloat16, jnp.float32
    dma = pltpu.SemaphoreType.DMA
    smem = pl.BlockSpec(memory_space=pltpu.SMEM)
    whole = pl.BlockSpec(memory_space=pl.ANY)
    return pl.pallas_call(
        functools.partial(kernel, place // NX, place % NX),
        out_shape=jax.ShapeDtypeStruct((rows, cols), bf16),
        in_specs=[smem] * 4 + [whole] * 4,
        out_specs=pl.BlockSpec(memory_space=pltpu.VMEM),
        scratch_shapes=[
            pltpu.VMEM((rows, width), bf16),
            pltpu.VMEM((n, HD), f32),
            pltpu.VMEM((n, HD), bf16),
            pltpu.VMEM(cache.shape, bf16),
            pltpu.VMEM((2, 2, keys, HD), bf16),
            pltpu.VMEM(w_out.shape, bf16),
            pltpu.VMEM((NZ, 2 * n, HD), bf16),
            pltpu.VMEM((NZ, 2 * n, HD), bf16),
            pltpu.VMEM((NZ, 8, HD), f32),
            pltpu.VMEM((n, HD), bf16),
            pltpu.VMEM((8, HD), f32),
            pltpu.VMEM((n, HD), f32),
            pltpu.VMEM((2, n, HD), f32),
            pltpu.VMEM((n, HD), f32),
            pltpu.VMEM((HD, HD), f32),
            pltpu.VMEM((NXH * NY, rows, cols), f32),
            pltpu.VMEM((NXH * NY, rows, cols), f32),
            dma((4,)),
            dma((2,)),
            dma((2,)),
            dma,
            dma((2 * NZ,)),
            dma((2 * NZ,)),
            dma((2 * NZ,)),
            dma,
            dma,
            dma((NXH * NY,)),
            dma((NXH * NY,)),
        ],
        compiler_params=pltpu.CompilerParams(
            collective_id=place, has_side_effects=True, vmem_limit_bytes=48 << 20
        ),
        name=f"attend_{place}",
    )(lengths, table, owner, readers, q, prefix, cache, w_out)


def shards(queries, prefix_kv, cache_kv, lengths, page_table, owner, readers, w_out):
    return lax.switch(
        owner[0] // NC,
        [functools.partial(attend, place) for place in range(NZ * NX)],
        queries,
        prefix_kv,
        cache_kv,
        lengths,
        page_table,
        owner,
        readers,
        w_out,
    )


def solution(mesh):
    placed = (
        P("dp", "tp"),
        P(None, "dp", "tp"),
        P(None, "dp", None, "tp"),
        P("dp"),
        P("dp", None),
        P(),
        P(),
        P("tp", None),
    )
    return jax.shard_map(
        shards, mesh=mesh, in_specs=placed, out_specs=P("dp", "tp"), check_vma=False
    )
```

```python
import functools
import math

import jax
import jax.numpy as jnp
from jax import lax
from jax.experimental import pallas as pl
from jax.experimental.pallas import tpu as pltpu
from jax.sharding import PartitionSpec as P

HD = 128
MESH = pl.DeviceIdType.MESH
LOG2E = math.log2(math.e)
LOW = -1e30
NZ, NX, NC, NY, NXH = 8, 2, 2, 4, 2
TP_STEPS = sorted(
    [(kx, ky) for kx in range(NXH) for ky in range(NY) if kx or ky],
    key=lambda k: -(2 * k[0] + min(k[1], NY - k[1])),
)


def nt_dot(a, b):
    return lax.dot_general(
        a, b, (((1,), (1,)), ((), ())), preferred_element_type=jnp.float32
    )


def kernel(
    oz,
    ox,
    lens_ref,
    table_ref,
    owner_ref,
    readers_ref,
    q_hbm,
    prefix_hbm,
    cache_hbm,
    w_hbm,
    out_ref,
    q_in,
    q_f32,
    q_rows,
    cache,
    kv,
    w,
    q_buf,
    o_send,
    s_send,
    o_recv,
    s_recv,
    num_res,
    ml_res,
    attn_f32,
    lse_f32,
    part_send,
    part_recv,
    local_sem,
    kv_send,
    kv_recv,
    q_send_sem,
    q_recv_sem,
    o_send_sem,
    s_send_sem,
    o_recv_sem,
    s_recv_sem,
    p_send_sem,
    p_recv_sem,
):
    dp, tp = lax.axis_index("dp"), lax.axis_index("tp")
    z, x, c = dp // 4, (dp // 2) % 2, dp % 2
    xh, y = tp // NY, tp % NY
    dz, dx = (z + NZ - oz) % NZ, (x + NX - ox) % NX
    here = dz * 2 + dx
    at_owner = here == 0
    rows = q_in.shape[0]
    heads = q_in.shape[1] // HD
    n = rows * heads
    pages, page = cache.shape[1], cache.shape[2]
    per = pages // rows
    c2 = LOG2E / HD**0.5

    def at(zz, xx, cc):
        return (zz * 4 + xx * 2 + cc, tp)

    def tp_peer(kx, ky):
        return (dp, ((xh + kx) % NXH) * NY + (y + ky) % NY)

    barrier = pltpu.get_barrier_semaphore()
    for k in TP_STEPS:
        pl.semaphore_signal(barrier, 1, device_id=tp_peer(*k), device_id_type=MESH)

    @pl.when(at_owner)
    def _():
        pl.semaphore_signal(barrier, 1, device_id=at(oz, ox, 1 - c), device_id_type=MESH)
        for i in range(2 * NZ - 1, 0, -1):
            pl.semaphore_signal(
                barrier,
                1,
                device_id=at((oz + i // 2) % NZ, (ox + i % 2) % NX, c),
                device_id_type=MESH,
            )

    load_q = pltpu.make_async_copy(q_hbm, q_in, local_sem.at[0])
    load_cache = pltpu.make_async_copy(cache_hbm, cache, local_sem.at[1])
    load_w = pltpu.make_async_copy(w_hbm, w, local_sem.at[2])
    load_kv = pltpu.make_async_copy(prefix_hbm, kv.at[0], local_sem.at[3])
    load_q.start()
    load_cache.start()

    @pl.when(at_owner)
    def _():
        load_kv.start()

    load_w.start()

    load_q.wait()
    for g in range(heads):
        q_f32[pl.ds(g, rows, stride=heads), :] = q_in[:, g * HD : (g + 1) * HD].astype(
            jnp.float32
        )
    q_rows[...] = q_f32[...].astype(jnp.bfloat16)

    def query_copy():
        return pltpu.make_async_remote_copy(
            q_rows,
            q_buf.at[dz, pl.ds(pl.multiple_of(dx * n, n), n)],
            q_send_sem,
            q_recv_sem.at[here],
            device_id=at(oz, ox, c),
            device_id_type=MESH,
        )

    @pl.when(jnp.logical_not(at_owner))
    def _():
        pl.semaphore_wait(barrier, len(TP_STEPS) + 1)
        query_copy().start()

    def kv_copy(i):
        return pltpu.make_async_remote_copy(
            prefix_hbm.at[i],
            kv.at[1, i],
            kv_send.at[i],
            kv_recv.at[i],
            device_id=at(oz, ox, 1 - c),
            device_id_type=MESH,
        )

    load_cache.wait()
    def resident(b, carry):
        mine = pl.ds(pl.multiple_of(b * heads, heads), heads)
        keys = jnp.concatenate(
            [cache[0, table_ref[0, b * per + j]] for j in range(per)], axis=0
        )
        s = nt_dot(q_f32[mine, :].astype(jnp.bfloat16), keys)
        pos = lax.broadcasted_iota(jnp.int32, s.shape, 1)
        s = jnp.where(pos < lens_ref[b], s, LOW)
        m = jnp.max(s, axis=-1, keepdims=True)
        e = jnp.exp2((s - m) * c2)
        values = jnp.concatenate(
            [cache[1, table_ref[0, b * per + j]] for j in range(per)], axis=0
        )
        ml_res[0, mine, :] = jnp.broadcast_to(m * c2, (heads, HD))
        ml_res[1, mine, :] = jnp.broadcast_to(
            jnp.sum(e, axis=-1, keepdims=True), (heads, HD)
        )
        num_res[mine, :] = jnp.dot(
            e.astype(jnp.bfloat16), values, preferred_element_type=jnp.float32
        )
        return carry

    lax.fori_loop(0, rows, resident, 0)

    @pl.when(at_owner)
    def _():
        pl.semaphore_wait(barrier, len(TP_STEPS) + 1)
        for i in range(2):
            kv_copy(i).start()
        q_buf[0, 0:n, :] = q_rows[...]
        load_kv.wait()
        for i in range(2):
            kv_copy(i).wait()
        source = (owner_ref[0] % NC + c) % 2

        def reply(zz, k, i):
            peer = at((oz + zz) % NZ, (ox + k) % NX, c)
            return (
                pltpu.make_async_remote_copy(
                    o_send.at[zz, pl.ds(k * n, n)],
                    o_recv,
                    o_send_sem.at[i],
                    o_recv_sem,
                    device_id=peer,
                    device_id_type=MESH,
                ),
                pltpu.make_async_remote_copy(
                    s_send.at[zz],
                    s_recv,
                    s_send_sem.at[i],
                    s_recv_sem,
                    device_id=peer,
                    device_id_type=MESH,
                ),
            )

        def arrival(zz, k):
            return pltpu.make_async_remote_copy(
                q_rows,
                q_buf.at[zz, pl.ds(k * n, n)],
                q_send_sem,
                q_recv_sem.at[zz * 2 + k],
                device_id=at(oz, ox, 1 - c),
                device_id_type=MESH,
            )

        def serve(t, carry):
            far = (t + 1) // 2
            zz = (t % 2) * far + (1 - t % 2) * ((NZ - far) % NZ)

            @pl.when(t > 0)
            def _():
                arrival(zz, 0).wait_recv()

            arrival(zz, 1).wait_recv()
            s = nt_dot(q_buf[zz], kv[source, 0])
            m = jnp.max(s, axis=-1, keepdims=True)
            e = jnp.exp2((s - m) * c2)
            total = jnp.sum(e, axis=-1, keepdims=True)
            num = jnp.dot(
                e.astype(jnp.bfloat16), kv[source, 1], preferred_element_type=jnp.float32
            )
            o_send[zz] = (num / total).astype(jnp.bfloat16)
            lse = m * c2 + jnp.log(total) * LOG2E
            s_send[zz] = jnp.transpose(jnp.broadcast_to(lse, (2 * n, HD)))[0:8, :]

            @pl.when(t > 0)
            def _():
                for copy in reply(zz, 0, zz * 2):
                    copy.start()

            for copy in reply(zz, 1, zz * 2 + 1):
                copy.start()
            return carry

        lax.fori_loop(0, NZ, serve, 0)
        o_recv[...] = o_send[0, 0:n, :]
        s_recv[...] = s_send[0]

        def settle(i, carry):
            for copy in reply(0, 0, i):
                copy.wait_send()
            return carry

        lax.fori_loop(1, 2 * NZ, settle, 0)

    @pl.when(jnp.logical_not(at_owner))
    def _():
        query_copy().wait_send()
        pltpu.make_async_remote_copy(
            o_recv, o_recv, o_send_sem.at[0], o_recv_sem, device_id=at(oz, ox, c), device_id_type=MESH
        ).wait_recv()
        pltpu.make_async_remote_copy(
            s_recv, s_recv, s_send_sem.at[0], s_recv_sem, device_id=at(oz, ox, c), device_id_type=MESH
        ).wait_recv()

    reads = readers_ref[0] == dp
    for i in range(1, readers_ref.shape[0]):
        reads = jnp.logical_or(reads, readers_ref[i] == dp)
    lse_f32[...] = jnp.transpose(jnp.broadcast_to(s_recv[0:1, :], (HD, HD)))
    lse = lse_f32[pl.ds(pl.multiple_of(dx * n, n), n), :]
    lse = jnp.where(reads, lse, LOW)
    m_res, l_res = ml_res[0], ml_res[1]
    top = jnp.maximum(m_res, lse)
    w_res, w_pre = jnp.exp2(m_res - top), jnp.exp2(lse - top)
    attn_f32[...] = (num_res[...] * w_res + o_recv[...].astype(jnp.float32) * w_pre) / (
        l_res * w_res + w_pre
    )
    attn = jnp.concatenate(
        [attn_f32[pl.ds(g, rows, stride=heads), :] for g in range(heads)], axis=1
    ).astype(jnp.bfloat16)

    load_w.wait()
    cols = out_ref.shape[1]

    def block(kx, ky):
        start = (((xh + kx) % NXH) * NY + (y + ky) % NY) * cols
        return jnp.dot(
            attn,
            w[:, pl.ds(pl.multiple_of(start, cols), cols)],
            preferred_element_type=jnp.float32,
        )

    def part_copy(kx, ky):
        i = kx * NY + ky
        return pltpu.make_async_remote_copy(
            part_send.at[i],
            part_recv.at[i],
            p_send_sem.at[i],
            p_recv_sem.at[i],
            device_id=tp_peer(kx, ky),
            device_id_type=MESH,
        )

    def project(i, carry):
        k = NXH * NY - 1 - i
        kx, ky = k // NY, k % NY
        part_send[k] = block(kx, ky)

        @pl.when(k > 0)
        def _():
            part_copy(kx, ky).start()

        return carry

    lax.fori_loop(0, NXH * NY, project, 0)
    total = part_send[0]
    for k in range(NXH * NY - 1, 0, -1):
        part_copy(k // NY, k % NY).wait_recv()
        total = total + part_recv[k]
    out_ref[...] = total.astype(out_ref.dtype)
    for k in range(1, NXH * NY):
        part_copy(k // NY, k % NY).wait_send()


def attend(place, q, prefix, cache, lengths, table, owner, readers, w_out):
    rows, width = q.shape
    n = rows * width // HD
    cols = w_out.shape[1] // (NXH * NY)
    keys = prefix.shape[1]
    bf16, f32 = jnp.bfloat16, jnp.float32
    dma = pltpu.SemaphoreType.DMA
    smem = pl.BlockSpec(memory_space=pltpu.SMEM)
    whole = pl.BlockSpec(memory_space=pl.ANY)
    return pl.pallas_call(
        functools.partial(kernel, place // NX, place % NX),
        out_shape=jax.ShapeDtypeStruct((rows, cols), bf16),
        in_specs=[smem] * 4 + [whole] * 4,
        out_specs=pl.BlockSpec(memory_space=pltpu.VMEM),
        scratch_shapes=[
            pltpu.VMEM((rows, width), bf16),
            pltpu.VMEM((n, HD), f32),
            pltpu.VMEM((n, HD), bf16),
            pltpu.VMEM(cache.shape, bf16),
            pltpu.VMEM((2, 2, keys, HD), bf16),
            pltpu.VMEM(w_out.shape, bf16),
            pltpu.VMEM((NZ, 2 * n, HD), bf16),
            pltpu.VMEM((NZ, 2 * n, HD), bf16),
            pltpu.VMEM((NZ, 8, HD), f32),
            pltpu.VMEM((n, HD), bf16),
            pltpu.VMEM((8, HD), f32),
            pltpu.VMEM((n, HD), f32),
            pltpu.VMEM((2, n, HD), f32),
            pltpu.VMEM((n, HD), f32),
            pltpu.VMEM((HD, HD), f32),
            pltpu.VMEM((NXH * NY, rows, cols), f32),
            pltpu.VMEM((NXH * NY, rows, cols), f32),
            dma((4,)),
            dma((2,)),
            dma((2,)),
            dma,
            dma((2 * NZ,)),
            dma((2 * NZ,)),
            dma((2 * NZ,)),
            dma,
            dma,
            dma((NXH * NY,)),
            dma((NXH * NY,)),
        ],
        compiler_params=pltpu.CompilerParams(
            collective_id=place, has_side_effects=True, vmem_limit_bytes=48 << 20
        ),
        name=f"attend_{place}",
    )(lengths, table, owner, readers, q, prefix, cache, w_out)


def shards(queries, prefix_kv, cache_kv, lengths, page_table, owner, readers, w_out):
    return lax.switch(
        owner[0] // NC,
        [functools.partial(attend, place) for place in range(NZ * NX)],
        queries,
        prefix_kv,
        cache_kv,
        lengths,
        page_table,
        owner,
        readers,
        w_out,
    )


def solution(mesh):
    placed = (
        P("dp", "tp"),
        P(None, "dp", "tp"),
        P(None, "dp", None, "tp"),
        P("dp"),
        P("dp", None),
        P(),
        P(),
        P("tp", None),
    )
    return jax.shard_map(
        shards, mesh=mesh, in_specs=placed, out_specs=P("dp", "tp"), check_vma=False
    )
```

```python
import functools
import math

import jax
import jax.numpy as jnp
from jax import lax
from jax.experimental import pallas as pl
from jax.experimental.pallas import tpu as pltpu
from jax.sharding import PartitionSpec as P

HD = 128
MESH = pl.DeviceIdType.MESH
LOG2E = math.log2(math.e)
LOW = -1e30
NZ, NX, NC, NY, NXH = 8, 2, 2, 4, 2
TP_STEPS = sorted(
    [(kx, ky) for kx in range(NXH) for ky in range(NY) if kx or ky],
    key=lambda k: -(2 * k[0] + min(k[1], NY - k[1])),
)


def nt_dot(a, b):
    return lax.dot_general(
        a, b, (((1,), (1,)), ((), ())), preferred_element_type=jnp.float32
    )


def kernel(
    oz,
    ox,
    lens_ref,
    table_ref,
    owner_ref,
    readers_ref,
    q_hbm,
    prefix_hbm,
    cache_hbm,
    w_hbm,
    out_ref,
    q_in,
    q_f32,
    q_rows,
    cache,
    kv,
    w,
    q_buf,
    o_send,
    s_send,
    o_recv,
    s_recv,
    num_res,
    ml_res,
    attn_f32,
    lse_f32,
    part_send,
    part_recv,
    local_sem,
    kv_send,
    kv_recv,
    q_send_sem,
    q_recv_sem,
    o_send_sem,
    s_send_sem,
    o_recv_sem,
    s_recv_sem,
    p_send_sem,
    p_recv_sem,
    known,
    clear,
):
    dp, tp = lax.axis_index("dp"), lax.axis_index("tp")
    z, x, c = dp // 4, (dp // 2) % 2, dp % 2
    xh, y = tp // NY, tp % NY
    dz, dx = (z + NZ - oz) % NZ, (x + NX - ox) % NX
    here = dz * 2 + dx
    at_owner = here == 0
    rows = q_in.shape[0]
    heads = q_in.shape[1] // HD
    n = rows * heads
    pages, page = cache.shape[1], cache.shape[2]
    per = pages // rows
    c2 = LOG2E / HD**0.5

    def at(zz, xx, cc):
        return (zz * 4 + xx * 2 + cc, tp)

    def tp_peer(kx, ky):
        return (dp, ((xh + kx) % NXH) * NY + (y + ky) % NY)

    barrier = pltpu.get_barrier_semaphore()
    beside = here == 1

    def greet_tp(sem):
        for k in TP_STEPS:
            pl.semaphore_signal(sem, 1, device_id=tp_peer(*k), device_id_type=MESH)

    @pl.when(at_owner)
    def _():
        pl.semaphore_signal(barrier, 1, device_id=at(oz, ox, 1 - c), device_id_type=MESH)
        for i in range(2 * NZ - 1, 0, -1):
            pl.semaphore_signal(
                barrier,
                1,
                device_id=at((oz + i // 2) % NZ, (ox + i % 2) % NX, c),
                device_id_type=MESH,
            )

    @pl.when(jnp.logical_not(at_owner))
    def _():
        greet_tp(barrier)

    load_q = pltpu.make_async_copy(q_hbm, q_in, local_sem.at[0])
    load_cache = pltpu.make_async_copy(cache_hbm, cache, local_sem.at[1])
    load_w = pltpu.make_async_copy(w_hbm, w, local_sem.at[2])
    load_kv = pltpu.make_async_copy(prefix_hbm, kv.at[0], local_sem.at[3])

    def kv_copy(i):
        return pltpu.make_async_remote_copy(
            prefix_hbm.at[i],
            kv.at[1, i],
            kv_send.at[i],
            kv_recv.at[i],
            device_id=at(oz, ox, 1 - c),
            device_id_type=MESH,
        )

    load_q.start()

    @pl.when(at_owner)
    def _():
        load_kv.start()
        pl.semaphore_wait(barrier, 1)
        for i in range(2):
            kv_copy(i).start()

    load_cache.start()
    load_w.start()

    load_q.wait()
    for g in range(heads):
        q_f32[pl.ds(g, rows, stride=heads), :] = q_in[:, g * HD : (g + 1) * HD].astype(
            jnp.float32
        )
    q_rows[...] = q_f32[...].astype(jnp.bfloat16)

    def query_copy():
        return pltpu.make_async_remote_copy(
            q_rows,
            q_buf.at[dz, pl.ds(pl.multiple_of(dx * n, n), n)],
            q_send_sem,
            q_recv_sem.at[here],
            device_id=at(oz, ox, c),
            device_id_type=MESH,
        )

    @pl.when(jnp.logical_not(at_owner))
    def _():
        pl.semaphore_wait(barrier, len(TP_STEPS) + 1)
        query_copy().start()

        @pl.when(beside)
        def _():
            greet_tp(known)
            pl.semaphore_wait(known, len(TP_STEPS))
            pl.semaphore_signal(clear, 1, device_id=at(oz, ox, c), device_id_type=MESH)

    load_cache.wait()

    def resident(b, carry):
        mine = pl.ds(pl.multiple_of(b * heads, heads), heads)
        keys = jnp.concatenate(
            [cache[0, table_ref[0, b * per + j]] for j in range(per)], axis=0
        )
        s = nt_dot(q_f32[mine, :].astype(jnp.bfloat16), keys)
        pos = lax.broadcasted_iota(jnp.int32, s.shape, 1)
        s = jnp.where(pos < lens_ref[b], s, LOW)
        m = jnp.max(s, axis=-1, keepdims=True)
        e = jnp.exp2((s - m) * c2)
        values = jnp.concatenate(
            [cache[1, table_ref[0, b * per + j]] for j in range(per)], axis=0
        )
        ml_res[0, mine, :] = jnp.broadcast_to(m * c2, (heads, HD))
        ml_res[1, mine, :] = jnp.broadcast_to(
            jnp.sum(e, axis=-1, keepdims=True), (heads, HD)
        )
        num_res[mine, :] = jnp.dot(
            e.astype(jnp.bfloat16), values, preferred_element_type=jnp.float32
        )
        return carry

    lax.fori_loop(0, rows, resident, 0)

    @pl.when(at_owner)
    def _():
        q_buf[0, 0:n, :] = q_rows[...]
        load_kv.wait()
        for i in range(2):
            kv_copy(i).wait()
        source = (owner_ref[0] % NC + c) % 2

        def reply(zz, k, i):
            peer = at((oz + zz) % NZ, (ox + k) % NX, c)
            return (
                pltpu.make_async_remote_copy(
                    o_send.at[zz, pl.ds(k * n, n)],
                    o_recv,
                    o_send_sem.at[i],
                    o_recv_sem,
                    device_id=peer,
                    device_id_type=MESH,
                ),
                pltpu.make_async_remote_copy(
                    s_send.at[zz],
                    s_recv,
                    s_send_sem.at[i],
                    s_recv_sem,
                    device_id=peer,
                    device_id_type=MESH,
                ),
            )

        def arrival(zz, k):
            return pltpu.make_async_remote_copy(
                q_rows,
                q_buf.at[zz, pl.ds(k * n, n)],
                q_send_sem,
                q_recv_sem.at[zz * 2 + k],
                device_id=at(oz, ox, 1 - c),
                device_id_type=MESH,
            )

        def serve(t, carry):
            far = (t + 1) // 2
            zz = (t % 2) * far + (1 - t % 2) * ((NZ - far) % NZ)

            @pl.when(t > 0)
            def _():
                arrival(zz, 0).wait_recv()

            arrival(zz, 1).wait_recv()
            s = nt_dot(q_buf[zz], kv[source, 0])
            m = jnp.max(s, axis=-1, keepdims=True)
            e = jnp.exp2((s - m) * c2)
            total = jnp.sum(e, axis=-1, keepdims=True)
            num = jnp.dot(
                e.astype(jnp.bfloat16), kv[source, 1], preferred_element_type=jnp.float32
            )
            o_send[zz] = (num / total).astype(jnp.bfloat16)
            lse = m * c2 + jnp.log(total) * LOG2E
            s_send[zz] = jnp.transpose(jnp.broadcast_to(lse, (2 * n, HD)))[0:8, :]

            @pl.when(t > 0)
            def _():
                for copy in reply(zz, 0, zz * 2):
                    copy.start()

            for copy in reply(zz, 1, zz * 2 + 1):
                copy.start()
            return carry

        lax.fori_loop(0, NZ, serve, 0)
        o_recv[...] = o_send[0, 0:n, :]
        s_recv[...] = s_send[0]

        def settle(i, carry):
            for copy in reply(0, 0, i):
                copy.wait_send()
            return carry

        lax.fori_loop(1, 2 * NZ, settle, 0)
        pl.semaphore_wait(clear, 1)

    @pl.when(jnp.logical_not(at_owner))
    def _():
        query_copy().wait_send()
        pltpu.make_async_remote_copy(
            o_recv, o_recv, o_send_sem.at[0], o_recv_sem, device_id=at(oz, ox, c), device_id_type=MESH
        ).wait_recv()
        pltpu.make_async_remote_copy(
            s_recv, s_recv, s_send_sem.at[0], s_recv_sem, device_id=at(oz, ox, c), device_id_type=MESH
        ).wait_recv()

    reads = readers_ref[0] == dp
    for i in range(1, readers_ref.shape[0]):
        reads = jnp.logical_or(reads, readers_ref[i] == dp)
    lse_f32[...] = jnp.transpose(jnp.broadcast_to(s_recv[0:1, :], (HD, HD)))
    lse = lse_f32[pl.ds(pl.multiple_of(dx * n, n), n), :]
    lse = jnp.where(reads, lse, LOW)
    m_res, l_res = ml_res[0], ml_res[1]
    top = jnp.maximum(m_res, lse)
    w_res, w_pre = jnp.exp2(m_res - top), jnp.exp2(lse - top)
    attn_f32[...] = (num_res[...] * w_res + o_recv[...].astype(jnp.float32) * w_pre) / (
        l_res * w_res + w_pre
    )
    attn = jnp.concatenate(
        [attn_f32[pl.ds(g, rows, stride=heads), :] for g in range(heads)], axis=1
    ).astype(jnp.bfloat16)

    load_w.wait()
    cols = out_ref.shape[1]

    def block(kx, ky):
        start = (((xh + kx) % NXH) * NY + (y + ky) % NY) * cols
        return jnp.dot(
            attn,
            w[:, pl.ds(pl.multiple_of(start, cols), cols)],
            preferred_element_type=jnp.float32,
        )

    def part_copy(kx, ky):
        i = kx * NY + ky
        return pltpu.make_async_remote_copy(
            part_send.at[i],
            part_recv.at[i],
            p_send_sem.at[i],
            p_recv_sem.at[i],
            device_id=tp_peer(kx, ky),
            device_id_type=MESH,
        )

    def project(i, carry):
        k = NXH * NY - 1 - i
        kx, ky = k // NY, k % NY
        part_send[k] = block(kx, ky)

        @pl.when(k > 0)
        def _():
            part_copy(kx, ky).start()

        return carry

    lax.fori_loop(0, NXH * NY, project, 0)
    total = part_send[0]
    for k in range(NXH * NY - 1, 0, -1):
        part_copy(k // NY, k % NY).wait_recv()
        total = total + part_recv[k]
    out_ref[...] = total.astype(out_ref.dtype)
    for k in range(1, NXH * NY):
        part_copy(k // NY, k % NY).wait_send()


def attend(place, q, prefix, cache, lengths, table, owner, readers, w_out):
    rows, width = q.shape
    n = rows * width // HD
    cols = w_out.shape[1] // (NXH * NY)
    keys = prefix.shape[1]
    bf16, f32 = jnp.bfloat16, jnp.float32
    dma = pltpu.SemaphoreType.DMA
    smem = pl.BlockSpec(memory_space=pltpu.SMEM)
    whole = pl.BlockSpec(memory_space=pl.ANY)
    return pl.pallas_call(
        functools.partial(kernel, place // NX, place % NX),
        out_shape=jax.ShapeDtypeStruct((rows, cols), bf16),
        in_specs=[smem] * 4 + [whole] * 4,
        out_specs=pl.BlockSpec(memory_space=pltpu.VMEM),
        scratch_shapes=[
            pltpu.VMEM((rows, width), bf16),
            pltpu.VMEM((n, HD), f32),
            pltpu.VMEM((n, HD), bf16),
            pltpu.VMEM(cache.shape, bf16),
            pltpu.VMEM((2, 2, keys, HD), bf16),
            pltpu.VMEM(w_out.shape, bf16),
            pltpu.VMEM((NZ, 2 * n, HD), bf16),
            pltpu.VMEM((NZ, 2 * n, HD), bf16),
            pltpu.VMEM((NZ, 8, HD), f32),
            pltpu.VMEM((n, HD), bf16),
            pltpu.VMEM((8, HD), f32),
            pltpu.VMEM((n, HD), f32),
            pltpu.VMEM((2, n, HD), f32),
            pltpu.VMEM((n, HD), f32),
            pltpu.VMEM((HD, HD), f32),
            pltpu.VMEM((NXH * NY, rows, cols), f32),
            pltpu.VMEM((NXH * NY, rows, cols), f32),
            dma((4,)),
            dma((2,)),
            dma((2,)),
            dma,
            dma((2 * NZ,)),
            dma((2 * NZ,)),
            dma((2 * NZ,)),
            dma,
            dma,
            dma((NXH * NY,)),
            dma((NXH * NY,)),
            pltpu.SemaphoreType.REGULAR,
            pltpu.SemaphoreType.REGULAR,
        ],
        compiler_params=pltpu.CompilerParams(
            collective_id=place, has_side_effects=True, vmem_limit_bytes=48 << 20
        ),
        name=f"attend_{place}",
    )(lengths, table, owner, readers, q, prefix, cache, w_out)


def shards(queries, prefix_kv, cache_kv, lengths, page_table, owner, readers, w_out):
    return lax.switch(
        lax.shift_right_logical(owner[0], 1),
        [functools.partial(attend, place) for place in range(NZ * NX)],
        queries,
        prefix_kv,
        cache_kv,
        lengths,
        page_table,
        owner,
        readers,
        w_out,
    )


def solution(mesh):
    placed = (
        P("dp", "tp"),
        P(None, "dp", "tp"),
        P(None, "dp", None, "tp"),
        P("dp"),
        P("dp", None),
        P(),
        P(),
        P("tp", None),
    )
    return jax.shard_map(
        shards, mesh=mesh, in_specs=placed, out_specs=P("dp", "tp"), check_vma=False
    )
```

```python
import functools
import math

import jax
import jax.numpy as jnp
from jax import lax
from jax.experimental import pallas as pl
from jax.experimental.pallas import tpu as pltpu
from jax.sharding import PartitionSpec as P

HD = 128
MESH = pl.DeviceIdType.MESH
LOG2E = math.log2(math.e)
LOW = -1e30
NZ, NX, NC, NY, NXH = 8, 2, 2, 4, 2
TP_STEPS = sorted(
    [(kx, ky) for kx in range(NXH) for ky in range(NY) if kx or ky],
    key=lambda k: -(2 * k[0] + min(k[1], NY - k[1])),
)


def nt_dot(a, b):
    return lax.dot_general(
        a, b, (((1,), (1,)), ((), ())), preferred_element_type=jnp.float32
    )


def kernel(
    oz,
    ox,
    lens_hbm,
    table_hbm,
    owner_hbm,
    readers_hbm,
    q_hbm,
    prefix_hbm,
    cache_hbm,
    w_hbm,
    out_ref,
    lens_ref,
    table_ref,
    owner_ref,
    readers_ref,
    q_in,
    q_f32,
    q_rows,
    cache,
    kv,
    w,
    q_buf,
    o_send,
    s_send,
    o_recv,
    s_recv,
    num_res,
    ml_res,
    attn_f32,
    lse_f32,
    part_send,
    part_recv,
    local_sem,
    kv_send,
    kv_recv,
    q_send_sem,
    q_recv_sem,
    o_send_sem,
    s_send_sem,
    o_recv_sem,
    s_recv_sem,
    p_send_sem,
    p_recv_sem,
    known,
    clear,
):
    dp, tp = lax.axis_index("dp"), lax.axis_index("tp")
    z, x, c = dp // 4, (dp // 2) % 2, dp % 2
    xh, y = tp // NY, tp % NY
    dz, dx = (z + NZ - oz) % NZ, (x + NX - ox) % NX
    here = dz * 2 + dx
    at_owner = here == 0
    rows = q_in.shape[0]
    heads = q_in.shape[1] // HD
    n = rows * heads
    pages, page = cache.shape[1], cache.shape[2]
    per = pages // rows
    c2 = LOG2E / HD**0.5

    def at(zz, xx, cc):
        return (zz * 4 + xx * 2 + cc, tp)

    def tp_peer(kx, ky):
        return (dp, ((xh + kx) % NXH) * NY + (y + ky) % NY)

    barrier = pltpu.get_barrier_semaphore()
    beside = here == 1

    def greet_tp(sem):
        for k in TP_STEPS:
            pl.semaphore_signal(sem, 1, device_id=tp_peer(*k), device_id_type=MESH)

    @pl.when(at_owner)
    def _():
        pl.semaphore_signal(barrier, 1, device_id=at(oz, ox, 1 - c), device_id_type=MESH)
        for i in range(2 * NZ - 1, 0, -1):
            pl.semaphore_signal(
                barrier,
                1,
                device_id=at((oz + i // 2) % NZ, (ox + i % 2) % NX, c),
                device_id_type=MESH,
            )

    @pl.when(jnp.logical_not(at_owner))
    def _():
        greet_tp(barrier)

    load_q = pltpu.make_async_copy(q_hbm, q_in, local_sem.at[0])
    load_cache = pltpu.make_async_copy(cache_hbm, cache, local_sem.at[1])
    load_w = pltpu.make_async_copy(w_hbm, w, local_sem.at[2])
    load_kv = pltpu.make_async_copy(prefix_hbm, kv.at[0], local_sem.at[3])

    def kv_copy(i):
        return pltpu.make_async_remote_copy(
            prefix_hbm.at[i],
            kv.at[1, i],
            kv_send.at[i],
            kv_recv.at[i],
            device_id=at(oz, ox, 1 - c),
            device_id_type=MESH,
        )

    load_scalars = [
        pltpu.make_async_copy(src, dst, local_sem.at[4 + i])
        for i, (src, dst) in enumerate(
            zip(
                (lens_hbm, table_hbm, owner_hbm, readers_hbm),
                (lens_ref, table_ref, owner_ref, readers_ref),
            )
        )
    ]
    load_q.start()
    for copy in load_scalars:
        copy.start()

    @pl.when(at_owner)
    def _():
        load_kv.start()
        pl.semaphore_wait(barrier, 1)
        for i in range(2):
            kv_copy(i).start()

    load_cache.start()
    load_w.start()

    load_q.wait()
    for g in range(heads):
        q_f32[pl.ds(g, rows, stride=heads), :] = q_in[:, g * HD : (g + 1) * HD].astype(
            jnp.float32
        )
    q_rows[...] = q_f32[...].astype(jnp.bfloat16)

    def query_copy():
        return pltpu.make_async_remote_copy(
            q_rows,
            q_buf.at[here],
            q_send_sem,
            q_recv_sem.at[here],
            device_id=at(oz, ox, c),
            device_id_type=MESH,
        )

    @pl.when(jnp.logical_not(at_owner))
    def _():
        pl.semaphore_wait(barrier, len(TP_STEPS) + 1)
        query_copy().start()

        @pl.when(beside)
        def _():
            greet_tp(known)
            pl.semaphore_wait(known, len(TP_STEPS))
            pl.semaphore_signal(clear, 1, device_id=at(oz, ox, c), device_id_type=MESH)

    for copy in load_scalars:
        copy.wait()
    load_cache.wait()

    def resident(b, carry):
        mine = pl.ds(pl.multiple_of(b * heads, heads), heads)
        keys = jnp.concatenate(
            [cache[0, table_ref[0, b * per + j]] for j in range(per)], axis=0
        )
        s = nt_dot(q_f32[mine, :].astype(jnp.bfloat16), keys)
        pos = lax.broadcasted_iota(jnp.int32, s.shape, 1)
        s = jnp.where(pos < lens_ref[b], s, LOW)
        m = jnp.max(s, axis=-1, keepdims=True)
        e = jnp.exp2((s - m) * c2)
        values = jnp.concatenate(
            [cache[1, table_ref[0, b * per + j]] for j in range(per)], axis=0
        )
        ml_res[0, mine, :] = jnp.broadcast_to(m * c2, (heads, HD))
        ml_res[1, mine, :] = jnp.broadcast_to(
            jnp.sum(e, axis=-1, keepdims=True), (heads, HD)
        )
        num_res[mine, :] = jnp.dot(
            e.astype(jnp.bfloat16), values, preferred_element_type=jnp.float32
        )
        return carry

    lax.fori_loop(0, rows, resident, 0)

    @pl.when(at_owner)
    def _():
        q_buf[0] = q_rows[...]
        load_kv.wait()
        for i in range(2):
            kv_copy(i).wait()
        source = (owner_ref[0] % NC + c) % 2

        def reply(i):
            peer = at((oz + i // 2) % NZ, (ox + i % 2) % NX, c)
            return (
                pltpu.make_async_remote_copy(
                    o_send.at[i],
                    o_recv,
                    o_send_sem,
                    o_recv_sem,
                    device_id=peer,
                    device_id_type=MESH,
                ),
                pltpu.make_async_remote_copy(
                    s_send.at[i],
                    s_recv,
                    s_send_sem,
                    s_recv_sem,
                    device_id=peer,
                    device_id_type=MESH,
                ),
            )

        def arrival(i):
            return pltpu.make_async_remote_copy(
                q_rows,
                q_buf.at[i],
                q_send_sem,
                q_recv_sem.at[i],
                device_id=at(oz, ox, 1 - c),
                device_id_type=MESH,
            )

        def serve(step, carry):
            za = (step + 1) % 4
            own = 1 - (za + 3) // 4
            zb = NZ - za - 4 * own
            ids = (za * 2, za * 2 + 1, zb * 2, zb * 2 + 1)

            @pl.when(own == 0)
            def _():
                arrival(ids[0]).wait_recv()

            for i in ids[1:]:
                arrival(i).wait_recv()
            q = jnp.concatenate([q_buf[i] for i in ids], axis=0)
            s = nt_dot(q, kv[source, 0])
            m = jnp.max(s, axis=-1, keepdims=True)
            e = jnp.exp2((s - m) * c2)
            total = jnp.sum(e, axis=-1, keepdims=True)
            num = jnp.dot(
                e.astype(jnp.bfloat16), kv[source, 1], preferred_element_type=jnp.float32
            )
            o = (num / total).astype(jnp.bfloat16)
            lse = jnp.broadcast_to(m * c2 + jnp.log(total) * LOG2E, (4 * n, HD))
            for j in range(2):
                row = jnp.transpose(lse[2 * n * j : 2 * n * (j + 1)])[0:8, :]
                s_send[ids[2 * j]] = row
                s_send[ids[2 * j + 1]] = row
            for j in range(4):
                o_send[ids[j]] = o[n * j : n * (j + 1)]
            for i in ids[:0:-1]:
                for copy in reply(i):
                    copy.start()

            @pl.when(own == 0)
            def _():
                for copy in reply(ids[0]):
                    copy.start()

            return carry

        lax.fori_loop(0, NZ // 2, serve, 0)
        o_recv[...] = o_send[0]
        s_recv[...] = s_send[0]
        for ref, sem in ((o_send, o_send_sem), (s_send, s_send_sem)):
            sent = ref.at[pl.ds(1, 2 * NZ - 1)]
            pltpu.make_async_remote_copy(
                sent, sent, sem, sem, device_id=at(oz, ox, 1 - c), device_id_type=MESH
            ).wait_send()
        pl.semaphore_wait(clear, 1)

    @pl.when(jnp.logical_not(at_owner))
    def _():
        query_copy().wait_send()
        pltpu.make_async_remote_copy(
            o_recv, o_recv, o_send_sem, o_recv_sem, device_id=at(oz, ox, c), device_id_type=MESH
        ).wait_recv()
        pltpu.make_async_remote_copy(
            s_recv, s_recv, s_send_sem, s_recv_sem, device_id=at(oz, ox, c), device_id_type=MESH
        ).wait_recv()

    reads = readers_ref[0] == dp
    for i in range(1, readers_ref.shape[0]):
        reads = jnp.logical_or(reads, readers_ref[i] == dp)
    lse_f32[...] = jnp.transpose(jnp.broadcast_to(s_recv[0:1, :], (HD, HD)))
    lse = lse_f32[pl.ds(pl.multiple_of(dx * n, n), n), :]
    lse = jnp.where(reads, lse, LOW)
    m_res, l_res = ml_res[0], ml_res[1]
    top = jnp.maximum(m_res, lse)
    w_res, w_pre = jnp.exp2(m_res - top), jnp.exp2(lse - top)
    attn_f32[...] = (num_res[...] * w_res + o_recv[...].astype(jnp.float32) * w_pre) / (
        l_res * w_res + w_pre
    )
    attn = jnp.concatenate(
        [attn_f32[pl.ds(g, rows, stride=heads), :] for g in range(heads)], axis=1
    ).astype(jnp.bfloat16)

    load_w.wait()
    cols = out_ref.shape[1]

    def block(kx, ky):
        start = (((xh + kx) % NXH) * NY + (y + ky) % NY) * cols
        return jnp.dot(
            attn,
            w[:, pl.ds(pl.multiple_of(start, cols), cols)],
            preferred_element_type=jnp.float32,
        )

    def part_copy(kx, ky):
        i = kx * NY + ky
        return pltpu.make_async_remote_copy(
            part_send.at[i],
            part_recv.at[i],
            p_send_sem,
            p_recv_sem,
            device_id=tp_peer(kx, ky),
            device_id_type=MESH,
        )

    def project(i, carry):
        kx, ky = 1 - i // NY, (i + 2) % NY
        k = kx * NY + ky
        part_send[k] = block(kx, ky)

        @pl.when(k > 0)
        def _():
            part_copy(kx, ky).start()

        return carry

    lax.fori_loop(0, NXH * NY, project, 0)
    others = pl.ds(1, NXH * NY - 1)
    whole = pltpu.make_async_remote_copy(
        part_send.at[others],
        part_recv.at[others],
        p_send_sem,
        p_recv_sem,
        device_id=tp_peer(0, 1),
        device_id_type=MESH,
    )
    whole.wait_recv()
    total = part_send[0]
    for k in range(1, NXH * NY):
        total = total + part_recv[k]
    out_ref[...] = total.astype(out_ref.dtype)
    whole.wait_send()


def attend(place, q, prefix, cache, lengths, table, owner, readers, w_out):
    rows, width = q.shape
    n = rows * width // HD
    cols = w_out.shape[1] // (NXH * NY)
    keys = prefix.shape[1]
    bf16, f32 = jnp.bfloat16, jnp.float32
    dma = pltpu.SemaphoreType.DMA
    whole = pl.BlockSpec(memory_space=pl.ANY)
    return pl.pallas_call(
        functools.partial(kernel, place // NX, place % NX),
        out_shape=jax.ShapeDtypeStruct((rows, cols), bf16),
        in_specs=[whole] * 8,
        out_specs=pl.BlockSpec(memory_space=pltpu.VMEM),
        scratch_shapes=[
            *(pltpu.SMEM(a.shape, a.dtype) for a in (lengths, table, owner, readers)),
            pltpu.VMEM((rows, width), bf16),
            pltpu.VMEM((n, HD), f32),
            pltpu.VMEM((n, HD), bf16),
            pltpu.VMEM(cache.shape, bf16),
            pltpu.VMEM((2, 2, keys, HD), bf16),
            pltpu.VMEM(w_out.shape, bf16),
            pltpu.VMEM((2 * NZ, n, HD), bf16),
            pltpu.VMEM((2 * NZ, n, HD), bf16),
            pltpu.VMEM((2 * NZ, 8, HD), f32),
            pltpu.VMEM((n, HD), bf16),
            pltpu.VMEM((8, HD), f32),
            pltpu.VMEM((n, HD), f32),
            pltpu.VMEM((2, n, HD), f32),
            pltpu.VMEM((n, HD), f32),
            pltpu.VMEM((HD, HD), f32),
            pltpu.VMEM((NXH * NY, rows, cols), f32),
            pltpu.VMEM((NXH * NY, rows, cols), f32),
            dma((8,)),
            dma((2,)),
            dma((2,)),
            dma,
            dma((2 * NZ,)),
            dma,
            dma,
            dma,
            dma,
            dma,
            dma,
            pltpu.SemaphoreType.REGULAR,
            pltpu.SemaphoreType.REGULAR,
        ],
        compiler_params=pltpu.CompilerParams(
            collective_id=place, has_side_effects=True, vmem_limit_bytes=48 << 20
        ),
        name=f"attend_{place}",
    )(lengths, table, owner, readers, q, prefix, cache, w_out)


def shards(queries, prefix_kv, cache_kv, lengths, page_table, owner, readers, w_out):
    return lax.switch(
        lax.shift_right_logical(owner[0], 1),
        [functools.partial(attend, place) for place in range(NZ * NX)],
        queries,
        prefix_kv,
        cache_kv,
        lengths,
        page_table,
        owner,
        readers,
        w_out,
    )


def solution(mesh):
    placed = (
        P("dp", "tp"),
        P(None, "dp", "tp"),
        P(None, "dp", None, "tp"),
        P("dp"),
        P("dp", None),
        P(),
        P(),
        P("tp", None),
    )
    return jax.shard_map(
        shards, mesh=mesh, in_specs=placed, out_specs=P("dp", "tp"), check_vma=False
    )
```

```python
import functools
import math

import jax
import jax.numpy as jnp
from jax import lax
from jax.experimental import pallas as pl
from jax.experimental.pallas import tpu as pltpu
from jax.sharding import PartitionSpec as P

HD = 128
MESH = pl.DeviceIdType.MESH
LOG2E = math.log2(math.e)
LOW = -1e30
NZ, NX, NC, NY, NXH = 8, 2, 2, 4, 2
TP_STEPS = sorted(
    [(kx, ky) for kx in range(NXH) for ky in range(NY) if kx or ky],
    key=lambda k: -(2 * k[0] + min(k[1], NY - k[1])),
)


def nt_dot(a, b):
    return lax.dot_general(
        a, b, (((1,), (1,)), ((), ())), preferred_element_type=jnp.float32
    )


def kernel(
    oz,
    ox,
    lens_hbm,
    table_hbm,
    owner_hbm,
    readers_hbm,
    q_hbm,
    prefix_hbm,
    cache_hbm,
    w_hbm,
    out_ref,
    lens_ref,
    table_ref,
    owner_ref,
    readers_ref,
    q_in,
    q_f32,
    q_rows,
    cache,
    kv,
    w,
    q_buf,
    o_send,
    o_recv,
    num_res,
    ml_res,
    attn_f32,
    lse_f32,
    part_send,
    part_recv,
    local_sem,
    kv_send,
    kv_recv,
    q_send_sem,
    q_recv_sem,
    o_send_sem,
    o_recv_sem,
    p_send_sem,
    p_recv_sem,
    go,
    known,
    clear,
):
    dp, tp = lax.axis_index("dp"), lax.axis_index("tp")
    z, x, c = dp // 4, (dp // 2) % 2, dp % 2
    xh, y = tp // NY, tp % NY
    dz, dx = (z + NZ - oz) % NZ, (x + NX - ox) % NX
    here = dz * 2 + dx
    at_owner = here == 0
    rows = q_in.shape[0]
    heads = q_in.shape[1] // HD
    n = rows * heads
    pages, page = cache.shape[1], cache.shape[2]
    per = pages // rows
    c2 = LOG2E / HD**0.5

    def at(zz, xx, cc):
        return (zz * 4 + xx * 2 + cc, tp)

    def tp_peer(kx, ky):
        return (dp, ((xh + kx) % NXH) * NY + (y + ky) % NY)

    barrier = pltpu.get_barrier_semaphore()
    beside = here == 1
    elsewhere = jnp.logical_not(at_owner)

    def greet_tp(sem):
        for k in TP_STEPS:
            pl.semaphore_signal(sem, 1, device_id=tp_peer(*k), device_id_type=MESH)

    pl.semaphore_signal(barrier, 1, device_id=at(z, x, 1 - c), device_id_type=MESH)

    @pl.when(at_owner)
    def _():
        for i in range(2 * NZ - 1, 0, -1):
            pl.semaphore_signal(
                barrier,
                1,
                device_id=at((oz + i // 2) % NZ, (ox + i % 2) % NX, 0),
                device_id_type=MESH,
            )

    @pl.when(jnp.logical_and(elsewhere, c == 1))
    def _():
        greet_tp(barrier)

    load_q = pltpu.make_async_copy(q_hbm, q_in, local_sem.at[0])
    load_cache = pltpu.make_async_copy(cache_hbm, cache, local_sem.at[1])
    load_w = pltpu.make_async_copy(w_hbm, w, local_sem.at[2])
    load_kv = pltpu.make_async_copy(prefix_hbm, kv.at[0], local_sem.at[3])

    def kv_copy(i):
        return pltpu.make_async_remote_copy(
            prefix_hbm.at[i],
            kv.at[1, i],
            kv_send.at[i],
            kv_recv.at[i],
            device_id=at(oz, ox, 1 - c),
            device_id_type=MESH,
        )

    load_scalars = [
        pltpu.make_async_copy(src, dst, local_sem.at[4 + i])
        for i, (src, dst) in enumerate(
            zip(
                (lens_hbm, table_hbm, owner_hbm, readers_hbm),
                (lens_ref, table_ref, owner_ref, readers_ref),
            )
        )
    ]
    load_q.start()
    for copy in load_scalars:
        copy.start()

    @pl.when(at_owner)
    def _():
        load_kv.start()
        pl.semaphore_wait(barrier, 1)
        for i in range(2):
            kv_copy(i).start()

    load_cache.start()
    load_w.start()

    load_q.wait()
    for g in range(heads):
        q_f32[pl.ds(g, rows, stride=heads), :] = q_in[:, g * HD : (g + 1) * HD].astype(
            jnp.float32
        )
    q_rows[...] = q_f32[...].astype(jnp.bfloat16)

    def query_copy():
        return pltpu.make_async_remote_copy(
            q_rows,
            q_buf.at[here],
            q_send_sem,
            q_recv_sem.at[here],
            device_id=at(oz, ox, c),
            device_id_type=MESH,
        )

    @pl.when(jnp.logical_and(elsewhere, c == 0))
    def _():
        pl.semaphore_wait(barrier, NC + 1)
        pl.semaphore_signal(go, 1, device_id=at(z, x, 1), device_id_type=MESH)
        query_copy().start()

    @pl.when(jnp.logical_and(elsewhere, c == 1))
    def _():
        pl.semaphore_wait(go, 1)
        query_copy().start()
        pl.semaphore_wait(barrier, len(TP_STEPS) + 1)
        greet_tp(known)
        pl.semaphore_wait(known, len(TP_STEPS))
        pl.semaphore_signal(clear, 1, device_id=at(z, x, 0), device_id_type=MESH)

        @pl.when(beside)
        def _():
            for core in range(NC):
                pl.semaphore_signal(
                    clear, 1, device_id=at(oz, ox, core), device_id_type=MESH
                )

    for copy in load_scalars:
        copy.wait()

    @pl.when(at_owner)
    def _():
        q_buf[0] = q_rows[...]
        load_kv.wait()
        for i in range(2):
            kv_copy(i).wait()
        source = (owner_ref[0] % NC + c) % 2

        def reply(i):
            return pltpu.make_async_remote_copy(
                o_send.at[i],
                o_recv,
                o_send_sem,
                o_recv_sem,
                device_id=at((oz + i // 2) % NZ, (ox + i % 2) % NX, c),
                device_id_type=MESH,
            )

        def arrival(i):
            return pltpu.make_async_remote_copy(
                q_rows,
                q_buf.at[i],
                q_send_sem,
                q_recv_sem.at[i],
                device_id=at(oz, ox, 1 - c),
                device_id_type=MESH,
            )

        def serve(step, carry):
            za = (step + 1) % 4
            own = 1 - (za + 3) // 4
            zb = NZ - za - 4 * own
            ids = (za * 2, za * 2 + 1, zb * 2, zb * 2 + 1)

            @pl.when(own == 0)
            def _():
                arrival(ids[0]).wait_recv()

            for i in ids[1:]:
                arrival(i).wait_recv()
            q = jnp.concatenate([q_buf[i] for i in ids], axis=0)
            s = nt_dot(q, kv[source, 0])
            m = jnp.max(s, axis=-1, keepdims=True)
            e = jnp.exp2((s - m) * c2)
            total = jnp.sum(e, axis=-1, keepdims=True)
            num = jnp.dot(
                e.astype(jnp.bfloat16), kv[source, 1], preferred_element_type=jnp.float32
            )
            o = (num / total).astype(jnp.bfloat16)
            lse = jnp.broadcast_to(m * c2 + jnp.log(total) * LOG2E, (4 * n, HD))
            line = lax.broadcasted_iota(jnp.int32, (8, HD), 0)
            for j in range(2):
                row = jnp.transpose(lse[2 * n * j : 2 * n * (j + 1)])[0:8, :]
                first = row.astype(jnp.bfloat16).astype(jnp.float32)
                second = (row - first).astype(jnp.bfloat16).astype(jnp.float32)
                terms = jnp.where(
                    line == 0, first, jnp.where(line == 1, second, row - first - second)
                )
                terms = jnp.concatenate([terms, terms], axis=0).astype(jnp.bfloat16)
                for k in range(2 * j, 2 * j + 2):
                    o_send[ids[k], n:, :] = terms
                    o_send[ids[k], 0:n, :] = o[n * k : n * (k + 1)]
            for i in ids[:0:-1]:
                reply(i).start()

            @pl.when(own == 0)
            def _():
                reply(ids[0]).start()

            return carry

        lax.fori_loop(0, NZ // 2, serve, 0)
        o_recv[...] = o_send[0]
        sent = o_send.at[pl.ds(1, 2 * NZ - 1)]
        pltpu.make_async_remote_copy(
            sent, sent, o_send_sem, o_recv_sem, device_id=at(oz, ox, 1 - c), device_id_type=MESH
        ).wait_send()

    load_cache.wait()

    def resident(b, carry):
        mine = pl.ds(pl.multiple_of(b * heads, heads), heads)
        keys = jnp.concatenate(
            [cache[0, table_ref[0, b * per + j]] for j in range(per)], axis=0
        )
        s = nt_dot(q_f32[mine, :].astype(jnp.bfloat16), keys)
        pos = lax.broadcasted_iota(jnp.int32, s.shape, 1)
        s = jnp.where(pos < lens_ref[b], s, LOW)
        m = jnp.max(s, axis=-1, keepdims=True)
        e = jnp.exp2((s - m) * c2)
        values = jnp.concatenate(
            [cache[1, table_ref[0, b * per + j]] for j in range(per)], axis=0
        )
        ml_res[0, mine, :] = jnp.broadcast_to(m * c2, (heads, HD))
        ml_res[1, mine, :] = jnp.broadcast_to(
            jnp.sum(e, axis=-1, keepdims=True), (heads, HD)
        )
        num_res[mine, :] = jnp.dot(
            e.astype(jnp.bfloat16), values, preferred_element_type=jnp.float32
        )
        return carry

    lax.fori_loop(0, rows, resident, 0)

    @pl.when(elsewhere)
    def _():
        query_copy().wait_send()
        pltpu.make_async_remote_copy(
            o_recv, o_recv, o_send_sem, o_recv_sem, device_id=at(oz, ox, c), device_id_type=MESH
        ).wait_recv()

    reads = readers_ref[0] == dp
    for i in range(1, readers_ref.shape[0]):
        reads = jnp.logical_or(reads, readers_ref[i] == dp)
    terms = o_recv[n:, :].astype(jnp.float32)
    row = terms[0:1] + terms[1:2] + terms[2:3]
    lse_f32[...] = jnp.transpose(jnp.broadcast_to(row, (HD, HD)))
    lse = lse_f32[pl.ds(pl.multiple_of(dx * n, n), n), :]
    lse = jnp.where(reads, lse, LOW)
    m_res, l_res = ml_res[0], ml_res[1]
    top = jnp.maximum(m_res, lse)
    w_res, w_pre = jnp.exp2(m_res - top), jnp.exp2(lse - top)
    attn_f32[...] = (num_res[...] * w_res + o_recv[0:n, :].astype(jnp.float32) * w_pre) / (
        l_res * w_res + w_pre
    )
    attn = jnp.concatenate(
        [attn_f32[pl.ds(g, rows, stride=heads), :] for g in range(heads)], axis=1
    ).astype(jnp.bfloat16)

    load_w.wait()
    cols = out_ref.shape[1]

    def part_copy(kx, ky):
        i = kx * NY + ky
        return pltpu.make_async_remote_copy(
            part_send.at[i],
            part_recv.at[i],
            p_send_sem,
            p_recv_sem,
            device_id=tp_peer(kx, ky),
            device_id_type=MESH,
        )

    @pl.when(jnp.logical_or(at_owner, c == 0))
    def _():
        pl.semaphore_wait(clear, 1)

    def project(i, carry):
        kx, pair = 1 - i // 2, (y // 2 + 1 + i % 2) % 2
        start = (((xh + kx) % NXH) * NY + pair * 2) * cols
        both = jnp.dot(
            attn,
            w[:, pl.ds(pl.multiple_of(start, 2 * cols), 2 * cols)],
            preferred_element_type=jnp.float32,
        )
        for j in range(2):
            ky = (pair * 2 + j + NY - y) % NY
            k = kx * NY + ky
            part_send[k] = both[:, j * cols : (j + 1) * cols]

            @pl.when(k > 0)
            def _(ky=ky):
                part_copy(kx, ky).start()

        return carry

    lax.fori_loop(0, NXH * NY // 2, project, 0)
    others = pl.ds(1, NXH * NY - 1)
    whole = pltpu.make_async_remote_copy(
        part_send.at[others],
        part_recv.at[others],
        p_send_sem,
        p_recv_sem,
        device_id=tp_peer(0, 1),
        device_id_type=MESH,
    )
    whole.wait_recv()
    total = part_send[0]
    for k in range(1, NXH * NY):
        total = total + part_recv[k]
    out_ref[...] = total.astype(out_ref.dtype)
    whole.wait_send()


def attend(place, q, prefix, cache, lengths, table, owner, readers, w_out):
    rows, width = q.shape
    n = rows * width // HD
    cols = w_out.shape[1] // (NXH * NY)
    keys = prefix.shape[1]
    bf16, f32 = jnp.bfloat16, jnp.float32
    dma = pltpu.SemaphoreType.DMA
    whole = pl.BlockSpec(memory_space=pl.ANY)
    return pl.pallas_call(
        functools.partial(kernel, place // NX, place % NX),
        out_shape=jax.ShapeDtypeStruct((rows, cols), bf16),
        in_specs=[whole] * 8,
        out_specs=pl.BlockSpec(memory_space=pltpu.VMEM),
        scratch_shapes=[
            *(pltpu.SMEM(a.shape, a.dtype) for a in (lengths, table, owner, readers)),
            pltpu.VMEM((rows, width), bf16),
            pltpu.VMEM((n, HD), f32),
            pltpu.VMEM((n, HD), bf16),
            pltpu.VMEM(cache.shape, bf16),
            pltpu.VMEM((2, 2, keys, HD), bf16),
            pltpu.VMEM(w_out.shape, bf16),
            pltpu.VMEM((2 * NZ, n, HD), bf16),
            pltpu.VMEM((2 * NZ, n + 16, HD), bf16),
            pltpu.VMEM((n + 16, HD), bf16),
            pltpu.VMEM((n, HD), f32),
            pltpu.VMEM((2, n, HD), f32),
            pltpu.VMEM((n, HD), f32),
            pltpu.VMEM((HD, HD), f32),
            pltpu.VMEM((NXH * NY, rows, cols), f32),
            pltpu.VMEM((NXH * NY, rows, cols), f32),
            dma((8,)),
            dma((2,)),
            dma((2,)),
            dma,
            dma((2 * NZ,)),
            dma,
            dma,
            dma,
            dma,
            pltpu.SemaphoreType.REGULAR,
            pltpu.SemaphoreType.REGULAR,
            pltpu.SemaphoreType.REGULAR,
        ],
        compiler_params=pltpu.CompilerParams(
            collective_id=place, has_side_effects=True, vmem_limit_bytes=48 << 20
        ),
        name=f"attend_{place}",
    )(lengths, table, owner, readers, q, prefix, cache, w_out)


def shards(queries, prefix_kv, cache_kv, lengths, page_table, owner, readers, w_out):
    return lax.switch(
        lax.shift_right_logical(owner[0], 1),
        [functools.partial(attend, place) for place in range(NZ * NX)],
        queries,
        prefix_kv,
        cache_kv,
        lengths,
        page_table,
        owner,
        readers,
        w_out,
    )


def solution(mesh):
    placed = (
        P("dp", "tp"),
        P(None, "dp", "tp"),
        P(None, "dp", None, "tp"),
        P("dp"),
        P("dp", None),
        P(),
        P(),
        P("tp", None),
    )
    return jax.shard_map(
        shards, mesh=mesh, in_specs=placed, out_specs=P("dp", "tp"), check_vma=False
    )
```

```python
import functools
import math

import jax
import jax.numpy as jnp
from jax import lax
from jax.experimental import pallas as pl
from jax.experimental.pallas import tpu as pltpu
from jax.sharding import PartitionSpec as P

HD = 128
MESH = pl.DeviceIdType.MESH
LOG2E = math.log2(math.e)
LOW = -1e30
NZ, NX, NC, NY, NXH = 8, 2, 2, 4, 2
TP_STEPS = sorted(
    [(kx, ky) for kx in range(NXH) for ky in range(NY) if kx or ky],
    key=lambda k: -(2 * k[0] + min(k[1], NY - k[1])),
)

PLACES = sorted(range(1, 2 * NZ), key=lambda i: -(min(i // 2, NZ - i // 2) + i % 2))


def nt_dot(a, b):
    return lax.dot_general(
        a, b, (((1,), (1,)), ((), ())), preferred_element_type=jnp.float32
    )


def kernel(
    oz,
    ox,
    lens_hbm,
    table_hbm,
    owner_hbm,
    readers_hbm,
    q_hbm,
    prefix_hbm,
    cache_hbm,
    w_hbm,
    out_ref,
    lens_ref,
    table_ref,
    owner_ref,
    readers_ref,
    q_in,
    q_f32,
    q_rows,
    cache,
    kv,
    w,
    q_buf,
    o_send,
    o_recv,
    num_res,
    ml_res,
    attn_f32,
    lse_f32,
    part_send,
    part_recv,
    local_sem,
    kv_send,
    kv_recv,
    q_send_sem,
    q_recv_sem,
    o_send_sem,
    o_recv_sem,
    p_send_sem,
    p_recv_sem,
    go,
    known,
    clear,
):
    dp, tp = lax.axis_index("dp"), lax.axis_index("tp")
    z, x, c = dp // 4, (dp // 2) % 2, dp % 2
    xh, y = tp // NY, tp % NY
    dz, dx = (z + NZ - oz) % NZ, (x + NX - ox) % NX
    here = dz * 2 + dx
    at_owner = here == 0
    rows = q_in.shape[0]
    heads = q_in.shape[1] // HD
    n = rows * heads
    pages, page = cache.shape[1], cache.shape[2]
    per = pages // rows
    c2 = LOG2E / HD**0.5

    def at(zz, xx, cc):
        return (zz * 4 + xx * 2 + cc, tp)

    def tp_peer(kx, ky):
        return (dp, ((xh + kx) % NXH) * NY + (y + ky) % NY)

    barrier = pltpu.get_barrier_semaphore()
    beside = here == 1
    elsewhere = jnp.logical_not(at_owner)

    def greet_tp(sem):
        for k in TP_STEPS:
            pl.semaphore_signal(sem, 1, device_id=tp_peer(*k), device_id_type=MESH)

    pl.semaphore_signal(barrier, 1, device_id=at(z, x, 1 - c), device_id_type=MESH)

    @pl.when(at_owner)
    def _():
        for i in PLACES:
            pl.semaphore_signal(
                barrier,
                1,
                device_id=at((oz + i // 2) % NZ, (ox + i % 2) % NX, 1),
                device_id_type=MESH,
            )

    @pl.when(jnp.logical_and(elsewhere, c == 0))
    def _():
        greet_tp(barrier)

    load_q = pltpu.make_async_copy(q_hbm, q_in, local_sem.at[0])
    load_cache = pltpu.make_async_copy(cache_hbm, cache, local_sem.at[1])
    load_w = pltpu.make_async_copy(w_hbm, w, local_sem.at[2])
    load_kv = pltpu.make_async_copy(prefix_hbm, kv.at[0], local_sem.at[3])

    def kv_copy(i):
        return pltpu.make_async_remote_copy(
            prefix_hbm.at[i],
            kv.at[1, i],
            kv_send.at[i],
            kv_recv.at[i],
            device_id=at(oz, ox, 1 - c),
            device_id_type=MESH,
        )

    load_scalars = [
        pltpu.make_async_copy(src, dst, local_sem.at[4 + i])
        for i, (src, dst) in enumerate(
            zip(
                (lens_hbm, table_hbm, owner_hbm, readers_hbm),
                (lens_ref, table_ref, owner_ref, readers_ref),
            )
        )
    ]
    load_q.start()
    for copy in load_scalars:
        copy.start()

    @pl.when(at_owner)
    def _():
        load_kv.start()
        pl.semaphore_wait(barrier, 1)
        for i in range(2):
            kv_copy(i).start()

    load_cache.start()
    load_w.start()

    load_q.wait()
    for g in range(heads):
        q_f32[pl.ds(g, rows, stride=heads), :] = q_in[:, g * HD : (g + 1) * HD].astype(
            jnp.float32
        )
    q_rows[...] = q_f32[...].astype(jnp.bfloat16)

    def query_copy():
        return pltpu.make_async_remote_copy(
            q_rows,
            q_buf.at[here],
            q_send_sem,
            q_recv_sem.at[here],
            device_id=at(oz, ox, 1 - c),
            device_id_type=MESH,
        )

    @pl.when(at_owner)
    def _():
        query_copy().start()

    @pl.when(jnp.logical_and(elsewhere, c == 1))
    def _():
        pl.semaphore_wait(barrier, NC + 1)
        pl.semaphore_signal(go, 1, device_id=at(z, x, 0), device_id_type=MESH)
        query_copy().start()

    @pl.when(jnp.logical_and(elsewhere, c == 0))
    def _():
        pl.semaphore_wait(go, 1)
        query_copy().start()
        pl.semaphore_wait(barrier, len(TP_STEPS) + 1)
        greet_tp(known)
        pl.semaphore_wait(known, len(TP_STEPS))
        pl.semaphore_signal(clear, 1, device_id=at(z, x, 1), device_id_type=MESH)

        @pl.when(beside)
        def _():
            for core in range(NC):
                pl.semaphore_signal(
                    clear, 1, device_id=at(oz, ox, core), device_id_type=MESH
                )

    for copy in load_scalars:
        copy.wait()

    @pl.when(at_owner)
    def _():
        load_kv.wait()
        for i in range(2):
            kv_copy(i).wait()
        source = (owner_ref[0] % NC + c) % 2

        def reply(i):
            return pltpu.make_async_remote_copy(
                o_send.at[i],
                o_recv,
                o_send_sem,
                o_recv_sem,
                device_id=at((oz + i // 2) % NZ, (ox + i % 2) % NX, 1 - c),
                device_id_type=MESH,
            )

        def arrival(i):
            return pltpu.make_async_remote_copy(
                q_rows,
                q_buf.at[i],
                q_send_sem,
                q_recv_sem.at[i],
                device_id=at(oz, ox, 1 - c),
                device_id_type=MESH,
            )

        def serve(step, carry):
            za = (step + 1) % 4
            own = 1 - (za + 3) // 4
            zb = NZ - za - 4 * own
            ids = (za * 2, za * 2 + 1, zb * 2, zb * 2 + 1)

            for i in ids:
                arrival(i).wait_recv()
            q = jnp.concatenate([q_buf[i] for i in ids], axis=0)
            s = nt_dot(q, kv[source, 0])
            m = jnp.max(s, axis=-1, keepdims=True)
            e = jnp.exp2((s - m) * c2)
            total = jnp.sum(e, axis=-1, keepdims=True)
            num = jnp.dot(
                e.astype(jnp.bfloat16), kv[source, 1], preferred_element_type=jnp.float32
            )
            o = (num / total).astype(jnp.bfloat16)
            lse = jnp.broadcast_to(m * c2 + jnp.log(total) * LOG2E, (4 * n, HD))
            line = lax.broadcasted_iota(jnp.int32, (8, HD), 0)
            for j in range(2):
                row = jnp.transpose(lse[2 * n * j : 2 * n * (j + 1)])[0:8, :]
                first = row.astype(jnp.bfloat16).astype(jnp.float32)
                second = (row - first).astype(jnp.bfloat16).astype(jnp.float32)
                terms = jnp.where(
                    line == 0, first, jnp.where(line == 1, second, row - first - second)
                )
                terms = jnp.concatenate([terms, terms], axis=0).astype(jnp.bfloat16)
                for k in range(2 * j, 2 * j + 2):
                    o_send[ids[k], n:, :] = terms
                    o_send[ids[k], 0:n, :] = o[n * k : n * (k + 1)]
            for i in ids[::-1]:
                reply(i).start()
            return carry

        lax.fori_loop(0, NZ // 2, serve, 0)
        pltpu.make_async_remote_copy(
            o_send, o_send, o_send_sem, o_recv_sem, device_id=at(oz, ox, 1 - c), device_id_type=MESH
        ).wait_send()

    load_cache.wait()

    def resident(b, carry):
        mine = pl.ds(pl.multiple_of(b * heads, heads), heads)
        keys = jnp.concatenate(
            [cache[0, table_ref[0, b * per + j]] for j in range(per)], axis=0
        )
        s = nt_dot(q_f32[mine, :].astype(jnp.bfloat16), keys)
        pos = lax.broadcasted_iota(jnp.int32, s.shape, 1)
        s = jnp.where(pos < lens_ref[b], s, LOW)
        m = jnp.max(s, axis=-1, keepdims=True)
        e = jnp.exp2((s - m) * c2)
        values = jnp.concatenate(
            [cache[1, table_ref[0, b * per + j]] for j in range(per)], axis=0
        )
        ml_res[0, mine, :] = jnp.broadcast_to(m * c2, (heads, HD))
        ml_res[1, mine, :] = jnp.broadcast_to(
            jnp.sum(e, axis=-1, keepdims=True), (heads, HD)
        )
        num_res[mine, :] = jnp.dot(
            e.astype(jnp.bfloat16), values, preferred_element_type=jnp.float32
        )
        return carry

    lax.fori_loop(0, rows, resident, 0)

    query_copy().wait_send()
    pltpu.make_async_remote_copy(
        o_recv, o_recv, o_send_sem, o_recv_sem, device_id=at(oz, ox, 1 - c), device_id_type=MESH
    ).wait_recv()

    reads = readers_ref[0] == dp
    for i in range(1, readers_ref.shape[0]):
        reads = jnp.logical_or(reads, readers_ref[i] == dp)
    terms = o_recv[n:, :].astype(jnp.float32)
    row = terms[0:1] + terms[1:2] + terms[2:3]
    lse_f32[...] = jnp.transpose(jnp.broadcast_to(row, (HD, HD)))
    lse = lse_f32[pl.ds(pl.multiple_of(dx * n, n), n), :]
    lse = jnp.where(reads, lse, LOW)
    m_res, l_res = ml_res[0], ml_res[1]
    top = jnp.maximum(m_res, lse)
    w_res, w_pre = jnp.exp2(m_res - top), jnp.exp2(lse - top)
    attn_f32[...] = (num_res[...] * w_res + o_recv[0:n, :].astype(jnp.float32) * w_pre) / (
        l_res * w_res + w_pre
    )
    attn = jnp.concatenate(
        [attn_f32[pl.ds(g, rows, stride=heads), :] for g in range(heads)], axis=1
    ).astype(jnp.bfloat16)

    load_w.wait()
    cols = out_ref.shape[1]

    def part_copy(kx, ky):
        i = kx * NY + ky
        return pltpu.make_async_remote_copy(
            part_send.at[i],
            part_recv.at[i],
            p_send_sem,
            p_recv_sem,
            device_id=tp_peer(kx, ky),
            device_id_type=MESH,
        )

    @pl.when(jnp.logical_or(at_owner, c == 1))
    def _():
        pl.semaphore_wait(clear, 1)

    def project(i, carry):
        kx, pair = 1 - i // 2, (y // 2 + 1 + i % 2) % 2
        start = (((xh + kx) % NXH) * NY + pair * 2) * cols
        both = jnp.dot(
            attn,
            w[:, pl.ds(pl.multiple_of(start, 2 * cols), 2 * cols)],
            preferred_element_type=jnp.float32,
        )
        for j in range(2):
            ky = (pair * 2 + j + NY - y) % NY
            k = kx * NY + ky
            part_send[k] = both[:, j * cols : (j + 1) * cols]

            @pl.when(k > 0)
            def _(ky=ky):
                part_copy(kx, ky).start()

        return carry

    lax.fori_loop(0, NXH * NY // 2, project, 0)
    others = pl.ds(1, NXH * NY - 1)
    whole = pltpu.make_async_remote_copy(
        part_send.at[others],
        part_recv.at[others],
        p_send_sem,
        p_recv_sem,
        device_id=tp_peer(0, 1),
        device_id_type=MESH,
    )
    whole.wait_recv()
    total = part_send[0]
    for k in range(1, NXH * NY):
        total = total + part_recv[k]
    out_ref[...] = total.astype(out_ref.dtype)
    whole.wait_send()


def attend(place, q, prefix, cache, lengths, table, owner, readers, w_out):
    rows, width = q.shape
    n = rows * width // HD
    cols = w_out.shape[1] // (NXH * NY)
    keys = prefix.shape[1]
    bf16, f32 = jnp.bfloat16, jnp.float32
    dma = pltpu.SemaphoreType.DMA
    whole = pl.BlockSpec(memory_space=pl.ANY)
    return pl.pallas_call(
        functools.partial(kernel, place // NX, place % NX),
        out_shape=jax.ShapeDtypeStruct((rows, cols), bf16),
        in_specs=[whole] * 8,
        out_specs=pl.BlockSpec(memory_space=pltpu.VMEM),
        scratch_shapes=[
            *(pltpu.SMEM(a.shape, a.dtype) for a in (lengths, table, owner, readers)),
            pltpu.VMEM((rows, width), bf16),
            pltpu.VMEM((n, HD), f32),
            pltpu.VMEM((n, HD), bf16),
            pltpu.VMEM(cache.shape, bf16),
            pltpu.VMEM((2, 2, keys, HD), bf16),
            pltpu.VMEM(w_out.shape, bf16),
            pltpu.VMEM((2 * NZ, n, HD), bf16),
            pltpu.VMEM((2 * NZ, n + 16, HD), bf16),
            pltpu.VMEM((n + 16, HD), bf16),
            pltpu.VMEM((n, HD), f32),
            pltpu.VMEM((2, n, HD), f32),
            pltpu.VMEM((n, HD), f32),
            pltpu.VMEM((HD, HD), f32),
            pltpu.VMEM((NXH * NY, rows, cols), f32),
            pltpu.VMEM((NXH * NY, rows, cols), f32),
            dma((8,)),
            dma((2,)),
            dma((2,)),
            dma,
            dma((2 * NZ,)),
            dma,
            dma,
            dma,
            dma,
            pltpu.SemaphoreType.REGULAR,
            pltpu.SemaphoreType.REGULAR,
            pltpu.SemaphoreType.REGULAR,
        ],
        compiler_params=pltpu.CompilerParams(
            collective_id=place, has_side_effects=True, vmem_limit_bytes=48 << 20
        ),
        name=f"attend_{place}",
    )(lengths, table, owner, readers, q, prefix, cache, w_out)


def shards(queries, prefix_kv, cache_kv, lengths, page_table, owner, readers, w_out):
    return lax.switch(
        lax.shift_right_logical(owner[0], 1),
        [functools.partial(attend, place) for place in range(NZ * NX)],
        queries,
        prefix_kv,
        cache_kv,
        lengths,
        page_table,
        owner,
        readers,
        w_out,
    )


def solution(mesh):
    placed = (
        P("dp", "tp"),
        P(None, "dp", "tp"),
        P(None, "dp", None, "tp"),
        P("dp"),
        P("dp", None),
        P(),
        P(),
        P("tp", None),
    )
    return jax.shard_map(
        shards, mesh=mesh, in_specs=placed, out_specs=P("dp", "tp"), check_vma=False
    )
```

```python
import functools
import math

import jax
import jax.numpy as jnp
from jax import lax
from jax.experimental import pallas as pl
from jax.experimental.pallas import tpu as pltpu
from jax.sharding import PartitionSpec as P

HD = 128
MESH = pl.DeviceIdType.MESH
LOG2E = math.log2(math.e)
LOW = -1e30
NZ, NX, NC, NY, NXH = 8, 2, 2, 4, 2
TP_STEPS = sorted(
    [(kx, ky) for kx in range(NXH) for ky in range(NY) if kx or ky],
    key=lambda k: -(2 * k[0] + min(k[1], NY - k[1])),
)

PLACES = sorted(range(1, 2 * NZ), key=lambda i: -(min(i // 2, NZ - i // 2) + i % 2))


def nt_dot(a, b):
    return lax.dot_general(
        a, b, (((1,), (1,)), ((), ())), preferred_element_type=jnp.float32
    )


def kernel(
    oz,
    ox,
    lens_hbm,
    table_hbm,
    owner_hbm,
    readers_hbm,
    q_hbm,
    prefix_hbm,
    cache_hbm,
    w_hbm,
    out_ref,
    lens_ref,
    table_ref,
    owner_ref,
    readers_ref,
    q_in,
    q_f32,
    q_rows,
    cache,
    kv,
    w,
    q_buf,
    o_send,
    o_recv,
    num_res,
    ml_res,
    attn_f32,
    lse_f32,
    part_send,
    part_recv,
    local_sem,
    kv_send,
    kv_recv,
    q_send_sem,
    q_recv_sem,
    o_send_sem,
    o_recv_sem,
    p_send_sem,
    p_recv_sem,
    go,
    known,
    clear,
):
    dp, tp = lax.axis_index("dp"), lax.axis_index("tp")
    z, x, c = dp // 4, (dp // 2) % 2, dp % 2
    xh, y = tp // NY, tp % NY
    dz, dx = (z + NZ - oz) % NZ, (x + NX - ox) % NX
    here = dz * 2 + dx
    at_owner = here == 0
    rows = q_in.shape[0]
    heads = q_in.shape[1] // HD
    n = rows * heads
    pages, page = cache.shape[1], cache.shape[2]
    per = pages // rows
    c2 = LOG2E / HD**0.5

    def at(zz, xx, cc):
        return (zz * 4 + xx * 2 + cc, tp)

    def tp_peer(kx, ky):
        return (dp, ((xh + kx) % NXH) * NY + (y + ky) % NY)

    barrier = pltpu.get_barrier_semaphore()
    beside = here == 1
    elsewhere = jnp.logical_not(at_owner)

    def greet_tp(sem):
        for k in TP_STEPS:
            pl.semaphore_signal(sem, 1, device_id=tp_peer(*k), device_id_type=MESH)

    pl.semaphore_signal(barrier, 1, device_id=at(z, x, 1 - c), device_id_type=MESH)

    @pl.when(at_owner)
    def _():
        for i in PLACES:
            pl.semaphore_signal(
                barrier,
                1,
                device_id=at((oz + i // 2) % NZ, (ox + i % 2) % NX, 1),
                device_id_type=MESH,
            )

    @pl.when(jnp.logical_and(elsewhere, c == 0))
    def _():
        greet_tp(barrier)

    load_q = pltpu.make_async_copy(q_hbm, q_in, local_sem.at[0])
    load_cache = pltpu.make_async_copy(cache_hbm, cache, local_sem.at[1])
    load_w = pltpu.make_async_copy(w_hbm, w, local_sem.at[2])
    load_kv = pltpu.make_async_copy(prefix_hbm, kv.at[0], local_sem.at[3])

    def kv_copy(i):
        return pltpu.make_async_remote_copy(
            prefix_hbm.at[i],
            kv.at[1, i],
            kv_send.at[i],
            kv_recv.at[i],
            device_id=at(oz, ox, 1 - c),
            device_id_type=MESH,
        )

    load_scalars = [
        pltpu.make_async_copy(src, dst, local_sem.at[4 + i])
        for i, (src, dst) in enumerate(
            zip(
                (lens_hbm, table_hbm, owner_hbm, readers_hbm),
                (lens_ref, table_ref, owner_ref, readers_ref),
            )
        )
    ]
    load_q.start()
    for copy in load_scalars:
        copy.start()

    @pl.when(at_owner)
    def _():
        load_kv.start()
        pl.semaphore_wait(barrier, 1)
        for i in range(2):
            kv_copy(i).start()

    load_cache.start()
    load_w.start()

    load_q.wait()
    for g in range(heads):
        q_f32[pl.ds(g, rows, stride=heads), :] = q_in[:, g * HD : (g + 1) * HD].astype(
            jnp.float32
        )
    q_rows[...] = q_f32[...].astype(jnp.bfloat16)

    def query_copy():
        return pltpu.make_async_remote_copy(
            q_rows,
            q_buf.at[here],
            q_send_sem,
            q_recv_sem.at[here],
            device_id=at(oz, ox, 1 - c),
            device_id_type=MESH,
        )

    @pl.when(at_owner)
    def _():
        query_copy().start()

    @pl.when(jnp.logical_and(elsewhere, c == 1))
    def _():
        pl.semaphore_wait(barrier, NC + 1)
        pl.semaphore_signal(go, 1, device_id=at(z, x, 0), device_id_type=MESH)
        query_copy().start()

    @pl.when(jnp.logical_and(elsewhere, c == 0))
    def _():
        pl.semaphore_wait(go, 1)
        query_copy().start()
        pl.semaphore_wait(barrier, len(TP_STEPS) + 1)
        greet_tp(known)
        pl.semaphore_wait(known, len(TP_STEPS))
        pl.semaphore_signal(clear, 1, device_id=at(z, x, 1), device_id_type=MESH)

        @pl.when(beside)
        def _():
            for core in range(NC):
                pl.semaphore_signal(
                    clear, 1, device_id=at(oz, ox, core), device_id_type=MESH
                )

    for copy in load_scalars:
        copy.wait()

    @pl.when(at_owner)
    def _():
        load_kv.wait()
        for i in range(2):
            kv_copy(i).wait()
        source = (owner_ref[0] % NC + c) % 2

        def reply(i):
            return pltpu.make_async_remote_copy(
                o_send.at[i],
                o_recv,
                o_send_sem,
                o_recv_sem,
                device_id=at((oz + i // 2) % NZ, (ox + i % 2) % NX, 1 - c),
                device_id_type=MESH,
            )

        def arrival(i):
            return pltpu.make_async_remote_copy(
                q_rows,
                q_buf.at[i],
                q_send_sem,
                q_recv_sem.at[i],
                device_id=at(oz, ox, 1 - c),
                device_id_type=MESH,
            )

        def order(step):
            if oz < 3:
                za = (step + 1) % 4
                return za, NZ - za - 4 * (1 - (za + 3) // 4)
            if oz <= NZ // 2:
                return step, NZ - 1 - step
            return (NZ - step) % NZ, step + 1

        def serve(step, carry):
            za, zb = order(step)
            ids = (za * 2, za * 2 + 1, zb * 2, zb * 2 + 1)

            for i in ids:
                arrival(i).wait_recv()
            q = jnp.concatenate([q_buf[i] for i in ids], axis=0)
            s = nt_dot(q, kv[source, 0])
            m = jnp.max(s, axis=-1, keepdims=True)
            e = jnp.exp2((s - m) * c2)
            total = jnp.sum(e, axis=-1, keepdims=True)
            num = jnp.dot(
                e.astype(jnp.bfloat16), kv[source, 1], preferred_element_type=jnp.float32
            )
            o = (num / total).astype(jnp.bfloat16)
            lse = jnp.broadcast_to(m * c2 + jnp.log(total) * LOG2E, (4 * n, HD))
            line = lax.broadcasted_iota(jnp.int32, (8, HD), 0)
            for j in range(2):
                row = jnp.transpose(lse[2 * n * j : 2 * n * (j + 1)])[0:8, :]
                first = row.astype(jnp.bfloat16).astype(jnp.float32)
                second = (row - first).astype(jnp.bfloat16).astype(jnp.float32)
                terms = jnp.where(
                    line == 0, first, jnp.where(line == 1, second, row - first - second)
                )
                terms = jnp.concatenate([terms, terms], axis=0).astype(jnp.bfloat16)
                for k in range(2 * j, 2 * j + 2):
                    o_send[ids[k], n:, :] = terms
                    o_send[ids[k], 0:n, :] = o[n * k : n * (k + 1)]
            for i in ids[::-1]:
                reply(i).start()
            return carry

        lax.fori_loop(0, NZ // 2, serve, 0)
        pltpu.make_async_remote_copy(
            o_send, o_send, o_send_sem, o_recv_sem, device_id=at(oz, ox, 1 - c), device_id_type=MESH
        ).wait_send()

    load_cache.wait()

    def resident(b, carry):
        mine = pl.ds(pl.multiple_of(b * heads, heads), heads)
        keys = jnp.concatenate(
            [cache[0, table_ref[0, b * per + j]] for j in range(per)], axis=0
        )
        s = nt_dot(q_f32[mine, :].astype(jnp.bfloat16), keys)
        pos = lax.broadcasted_iota(jnp.int32, s.shape, 1)
        s = jnp.where(pos < lens_ref[b], s, LOW)
        m = jnp.max(s, axis=-1, keepdims=True)
        e = jnp.exp2((s - m) * c2)
        values = jnp.concatenate(
            [cache[1, table_ref[0, b * per + j]] for j in range(per)], axis=0
        )
        ml_res[0, mine, :] = jnp.broadcast_to(m * c2, (heads, HD))
        ml_res[1, mine, :] = jnp.broadcast_to(
            jnp.sum(e, axis=-1, keepdims=True), (heads, HD)
        )
        num_res[mine, :] = jnp.dot(
            e.astype(jnp.bfloat16), values, preferred_element_type=jnp.float32
        )
        return carry

    lax.fori_loop(0, rows, resident, 0)

    query_copy().wait_send()
    pltpu.make_async_remote_copy(
        o_recv, o_recv, o_send_sem, o_recv_sem, device_id=at(oz, ox, 1 - c), device_id_type=MESH
    ).wait_recv()

    reads = readers_ref[0] == dp
    for i in range(1, readers_ref.shape[0]):
        reads = jnp.logical_or(reads, readers_ref[i] == dp)
    terms = o_recv[n:, :].astype(jnp.float32)
    row = terms[0:1] + terms[1:2] + terms[2:3]
    lse_f32[...] = jnp.transpose(jnp.broadcast_to(row, (HD, HD)))
    lse = lse_f32[pl.ds(pl.multiple_of(dx * n, n), n), :]
    lse = jnp.where(reads, lse, LOW)
    m_res, l_res = ml_res[0], ml_res[1]
    top = jnp.maximum(m_res, lse)
    w_res, w_pre = jnp.exp2(m_res - top), jnp.exp2(lse - top)
    attn_f32[...] = (num_res[...] * w_res + o_recv[0:n, :].astype(jnp.float32) * w_pre) / (
        l_res * w_res + w_pre
    )
    attn = jnp.concatenate(
        [attn_f32[pl.ds(g, rows, stride=heads), :] for g in range(heads)], axis=1
    ).astype(jnp.bfloat16)

    load_w.wait()
    cols = out_ref.shape[1]

    def part_copy(kx, ky):
        i = kx * NY + ky
        return pltpu.make_async_remote_copy(
            part_send.at[i],
            part_recv.at[i],
            p_send_sem,
            p_recv_sem,
            device_id=tp_peer(kx, ky),
            device_id_type=MESH,
        )

    @pl.when(jnp.logical_or(at_owner, c == 1))
    def _():
        pl.semaphore_wait(clear, 1)

    def project(i, carry):
        kx, pair = 1 - i // 2, (y // 2 + 1 + i % 2) % 2
        start = (((xh + kx) % NXH) * NY + pair * 2) * cols
        both = jnp.dot(
            attn,
            w[:, pl.ds(pl.multiple_of(start, 2 * cols), 2 * cols)],
            preferred_element_type=jnp.float32,
        )
        for j in range(2):
            ky = (pair * 2 + j + NY - y) % NY
            k = kx * NY + ky
            part_send[k] = both[:, j * cols : (j + 1) * cols]

            @pl.when(k > 0)
            def _(ky=ky):
                part_copy(kx, ky).start()

        return carry

    lax.fori_loop(0, NXH * NY // 2, project, 0)
    others = pl.ds(1, NXH * NY - 1)
    whole = pltpu.make_async_remote_copy(
        part_send.at[others],
        part_recv.at[others],
        p_send_sem,
        p_recv_sem,
        device_id=tp_peer(0, 1),
        device_id_type=MESH,
    )
    whole.wait_recv()
    total = part_send[0]
    for k in range(1, NXH * NY):
        total = total + part_recv[k]
    out_ref[...] = total.astype(out_ref.dtype)
    whole.wait_send()


def attend(place, q, prefix, cache, lengths, table, owner, readers, w_out):
    rows, width = q.shape
    n = rows * width // HD
    cols = w_out.shape[1] // (NXH * NY)
    keys = prefix.shape[1]
    bf16, f32 = jnp.bfloat16, jnp.float32
    dma = pltpu.SemaphoreType.DMA
    whole = pl.BlockSpec(memory_space=pl.ANY)
    return pl.pallas_call(
        functools.partial(kernel, place // NX, place % NX),
        out_shape=jax.ShapeDtypeStruct((rows, cols), bf16),
        in_specs=[whole] * 8,
        out_specs=pl.BlockSpec(memory_space=pltpu.VMEM),
        scratch_shapes=[
            *(pltpu.SMEM(a.shape, a.dtype) for a in (lengths, table, owner, readers)),
            pltpu.VMEM((rows, width), bf16),
            pltpu.VMEM((n, HD), f32),
            pltpu.VMEM((n, HD), bf16),
            pltpu.VMEM(cache.shape, bf16),
            pltpu.VMEM((2, 2, keys, HD), bf16),
            pltpu.VMEM(w_out.shape, bf16),
            pltpu.VMEM((2 * NZ, n, HD), bf16),
            pltpu.VMEM((2 * NZ, n + 16, HD), bf16),
            pltpu.VMEM((n + 16, HD), bf16),
            pltpu.VMEM((n, HD), f32),
            pltpu.VMEM((2, n, HD), f32),
            pltpu.VMEM((n, HD), f32),
            pltpu.VMEM((HD, HD), f32),
            pltpu.VMEM((NXH * NY, rows, cols), f32),
            pltpu.VMEM((NXH * NY, rows, cols), f32),
            dma((8,)),
            dma((2,)),
            dma((2,)),
            dma,
            dma((2 * NZ,)),
            dma,
            dma,
            dma,
            dma,
            pltpu.SemaphoreType.REGULAR,
            pltpu.SemaphoreType.REGULAR,
            pltpu.SemaphoreType.REGULAR,
        ],
        compiler_params=pltpu.CompilerParams(
            collective_id=place, has_side_effects=True, vmem_limit_bytes=48 << 20
        ),
        name=f"attend_{place}",
    )(lengths, table, owner, readers, q, prefix, cache, w_out)


def shards(queries, prefix_kv, cache_kv, lengths, page_table, owner, readers, w_out):
    return lax.switch(
        lax.shift_right_logical(owner[0], 1),
        [functools.partial(attend, place) for place in range(NZ * NX)],
        queries,
        prefix_kv,
        cache_kv,
        lengths,
        page_table,
        owner,
        readers,
        w_out,
    )


def solution(mesh):
    placed = (
        P("dp", "tp"),
        P(None, "dp", "tp"),
        P(None, "dp", None, "tp"),
        P("dp"),
        P("dp", None),
        P(),
        P(),
        P("tp", None),
    )
    return jax.shard_map(
        shards, mesh=mesh, in_specs=placed, out_specs=P("dp", "tp"), check_vma=False
    )
```
